32 devices in a mesh: seg: 2 (over y), bank: 16 (over z, x, core).
Axes of the slice: x: 2, y: 2, z: 4, core: 2. Of those that a mesh axis runs over, the one named last changes fastest.
Arguments:
- strain: float32 [4, 2, 262144], P('seg', None, 'bank'), may hold values from -6 to 6
- templates: bfloat16 [64, 2, 262144], P('bank'), may hold values from -6 to 6
- counts: int32 [16], P('bank'), may hold values from 1 to 4, 24 in all
- edges: int32 [64, 17], P('bank'), may hold values from 1 to 262144, as said below
Outputs:
- slot_peak: float32 [64, 4], P('bank', 'seg')
- segment_peak: float32 [4], P('seg')
The draws below stay inside these ranges and needn't reach their ends.
Inputs may be any that keep to these rules, and one draw needn't show every extreme that they name: counts[b] is the number of live slots of shard b, which are its first ones; some shard has all 4 slots live. Each row of edges rises strictly; its first and last edges lie more than 114688 bins apart, and each band holds about a 64th of that span or more.
All inputs are finite; a program needn't handle non-finite values.
Results may differ from the reference program's by a relative error of at most 0.0003.
Values may be sent and summed in bfloat16 or wider, within the bound.
No kernel may reach another device: no remote copies, remote signals or barrier semaphores. Data moves between devices by JAX's collectives and lax.ppermute only.
A program may use at most 128 MiB of HBM per device.

```python
import math
import jax
import jax.numpy as jnp
import numpy as np
from jax import lax

CAP = 4
SAMPLES = 524288
CELL = 128
BINS = 16
FREQS = 262144
CELLS = 4096
SEGMENTS = 4
SLOTS = 64
N_BANK = 16


def draw_edges(key, part):
    first_key = jax.random.fold_in(key, 11)
    last_key = jax.random.fold_in(key, 23)
    width_key = jax.random.fold_in(key, 37)
    first = jnp.maximum(1, jax.random.randint(first_key, (SLOTS,), -(FREQS // 64), FREQS // 16))
    last = jnp.minimum(FREQS, jax.random.randint(last_key, (SLOTS,), FREQS // 2, FREQS + FREQS // 4))
    widths = jax.random.randint(width_key, (SLOTS, BINS), 1, 5)
    running = jnp.concatenate([jnp.zeros((SLOTS, 1), jnp.int32), jnp.cumsum(widths, axis=1).astype(jnp.int32)], axis=1)
    span = last - first
    result = first[:, None] + span[:, None] * running // running[:, BINS:BINS + 1]
    return result.astype(jnp.int32)


def level_of(key, extent, cuts, low, top_value):
    gain = 1.0
    for dim, blocks in cuts:
        steps = jax.random.uniform(jax.random.fold_in(jax.random.fold_in(key, 6), dim), (blocks,), jnp.float32, low / len(cuts), top_value / len(cuts))
        gain = gain * jnp.repeat(jnp.exp(steps), extent[dim] // blocks).reshape((-1,) + (1,) * (len(extent) - 1 - dim))
    return gain


def profile(amount, total, reach, lean):
    weights = [(1 << 20) // math.isqrt(grade ** lean) + 1 for grade in range(2, amount + 1)]
    spare, holding = total - reach - (amount - 1), [1] * (amount - 1)
    while spare > 0:
        free = [i for i in range(amount - 1) if holding[i] < reach]
        whole, budget = sum([weights[i] for i in free]), spare
        for i in free:
            more = min(reach - holding[i], max(1, budget * weights[i] // whole), spare)
            holding[i] = holding[i] + more
            spare = spare - more
    return np.array([reach] + holding)


def uneven_parts(rng, count, total, reach, lean):
    if count == 2:
        one = jax.random.randint(rng, (), max(1, total - reach), min(reach, total - 1) + 1)
        return jnp.stack([one, total - one])
    lengths = jnp.asarray(profile(count, total, reach, lean), jnp.int32)
    twos = (count - 1) // 2
    giver, sink = lengths[1:1 + 2 * twos:2], lengths[2:2 + 2 * twos:2]
    margin = jnp.minimum(giver - 1, reach - sink)
    moved = jax.random.randint(jax.random.fold_in(rng, 1), (twos,), 0, 1 << 20) % (margin + 1)
    lengths = lengths.at[1:1 + 2 * twos:2].set(giver - moved).at[2:2 + 2 * twos:2].set(sink + moved)
    return lengths[jax.random.permutation(jax.random.fold_in(rng, 2), count)]


def normal_values(key, dims, scale, reach, shards=(), kind=jnp.bfloat16):
    drawn = scale * jax.random.normal(key, dims, jnp.float32)
    if shards:
        drawn = drawn * level_of(key, dims, shards, -0.22, 0.18)
    return jnp.clip(drawn, -reach, reach).astype(kind)


def setup_inputs(seed: int = 0) -> dict:
    keys = jax.random.split(jax.random.key(seed), 5)
    return {
        "strain": normal_values(keys[0], (SEGMENTS, 2, FREQS), 1.0, 6.0, ((0, 2), (2, 16)), jnp.float32),
        "templates": normal_values(keys[1], (SLOTS, 2, FREQS), 1.0, 6.0, ((0, 16),)),
        "counts": uneven_parts(keys[2], N_BANK, SLOTS * 3 // 8, CAP, 2).astype(jnp.int32),
        "edges": draw_edges(jax.random.fold_in(keys[4], 71), 0),
    }


EPSILON = 1e-06

def pair_peak(spectrum, template, edge_row):
    index = jnp.arange(FREQS, dtype=jnp.int32)
    inside = (index >= edge_row[0]) & (index < edge_row[BINS])
    wave_real = template[0].astype(jnp.float32)
    wave_imag = template[1].astype(jnp.float32)
    data_real = spectrum[0]
    data_imag = spectrum[1]
    product_real = jnp.where(inside, data_real * wave_real + data_imag * wave_imag, 0.0)
    product_imag = jnp.where(inside, data_imag * wave_real - data_real * wave_imag, 0.0)
    power = jnp.where(inside, wave_real * wave_real + wave_imag * wave_imag, 0.0)
    band = lax.optimization_barrier(jnp.sum((index[:, None] >= edge_row[None, :]).astype(jnp.int32), axis=1)) - 1
    band = jnp.clip(band, 0, BINS - 1).astype(jnp.int32)
    band_power = jax.ops.segment_sum(power, band, num_segments=BINS)
    energy = jnp.sum(power)
    product = product_real + 1j * product_imag
    padded = jnp.concatenate([product, jnp.zeros_like(product)])
    series = jnp.fft.ifft(padded) * SAMPLES
    loudness = jnp.abs(series) / jnp.sqrt(energy)
    cell_loud = lax.optimization_barrier(jnp.max(loudness.reshape(CELLS, CELL), axis=1))
    folded_id = (band * CELLS + index % CELLS).astype(jnp.int32)
    folded = jax.ops.segment_sum(product, folded_id, num_segments=BINS * CELLS).reshape(BINS, CELLS)
    bands = jnp.fft.ifft(folded, axis=1) * CELLS
    total = lax.optimization_barrier(jnp.sum(bands, axis=0))
    weight = band_power / energy
    deviation = bands - weight[:, None] * total[None, :]
    misfit = lax.optimization_barrier(jnp.sum(jnp.abs(deviation) ** 2 / (band_power[:, None] + EPSILON), axis=0))
    reduced = misfit / (2 * BINS - 2)
    factor = jnp.where(reduced > 1.0, ((1.0 + reduced ** 3) / 2.0) ** (-1.0 / 6.0), 1.0)
    return jnp.max(cell_loud * factor)

def reference(strain, templates, counts, edges):

    def per_slot(item):
        template, edge_row = item
        return jnp.stack([pair_peak(strain[segment], template, edge_row) for segment in range(SEGMENTS)])
    peaks = lax.map(per_slot, (templates, edges))
    live = jnp.arange(SLOTS, dtype=jnp.int32) % CAP < jnp.repeat(counts, CAP)
    slot_peak = jnp.where(live[:, None], peaks, 0.0)
    return (slot_peak, lax.optimization_barrier(jnp.max(slot_peak, axis=0)))
```

```python
import numpy as np

import jax
import jax.numpy as jnp
from jax import lax
from jax.experimental import pallas as pl
from jax.experimental.pallas import tpu as pltpu
from jax.sharding import PartitionSpec as P

CELL = 128
BINS = 16
EPSILON = 1e-06
ROWS = 512
HALF = 256
QUART = 128
CHUNK = 32


def split_bf16(x):
    high = x.astype(jnp.bfloat16)
    low = (x - high.astype(jnp.float32)).astype(jnp.bfloat16)
    return high, low


def host_split(x):
    high = x.astype(np.float32).astype(jnp.bfloat16)
    low = (x - high.astype(np.float64)).astype(np.float32).astype(jnp.bfloat16)
    return high, low


def host_tables():
    k = np.arange(HALF)
    u = np.arange(QUART) + 0.5
    angle = 2 * np.pi * u[:, None] * k[None, :] / HALF
    wave = np.concatenate([np.cos(angle), np.sin(angle)], axis=0)
    high, low = host_split(wave)
    first = np.concatenate([high, high, low], axis=1)
    second = np.concatenate([high.T, high.T, low.T], axis=0)
    eight = 2 * np.pi * (np.arange(8)[:, None] * np.arange(8)[None, :] % 8) / 8
    block = np.block([[np.cos(eight), -np.sin(eight)], [np.sin(eight), np.cos(eight)]])
    high, low = host_split(block)
    octet = np.concatenate([high, high, low], axis=1)
    angle = 2 * np.pi * k[None, :] * np.array([-2, -1, 1])[:, None] / 1024
    rows = np.stack([np.cos(angle), np.sin(angle)], axis=1)
    rows = np.broadcast_to(rows[..., None], rows.shape + (128,)).astype(np.float32)
    t0 = np.stack([np.stack([4 * np.arange(QUART) + v, 4 * (255 - np.arange(QUART)) + v]) for v in range(4)])
    angle = 2 * np.pi * ((t0[..., None] * np.arange(ROWS)) % (1 << 19)) / (1 << 19)
    between = np.stack([np.cos(angle), np.sin(angle)], axis=2).astype(np.float32)
    angle = 2 * np.pi * (128 * np.arange(8)[:, None] * np.arange(ROWS)[None, :]) / (1 << 19)
    coarse = np.stack([np.cos(angle), np.sin(angle)]).astype(np.float32)
    angle = -2 * np.pi * k / ROWS
    lanes = np.stack([np.cos(angle), np.sin(angle)]).astype(np.float32)
    lanes = np.broadcast_to(lanes[:, None, :], (2, 8, HALF)).copy()
    return first, second, octet, rows.copy(), between, coarse, lanes


def lane_butterfly(real, imag, lanes_real, lanes_imag):
    low_r, high_r = real[:, :HALF], real[:, HALF:]
    low_i, high_i = imag[:, :HALF], imag[:, HALF:]
    sum_r, sum_i = low_r + high_r, low_i + high_i
    even_r = sum_r * lanes_real - sum_i * lanes_imag
    even_i = sum_r * lanes_imag + sum_i * lanes_real
    return even_r, even_i, low_r - high_r, low_i - high_i


def split_dot(high, low, second_ref):
    return jnp.dot(
        jnp.concatenate([high, low, high], axis=1), second_ref[...], preferred_element_type=jnp.float32
    )


def make_kernel(slots):
    def kernel(
        plan_ref, edge_ref, strain_ref, wave_ref, first_ref, second_ref, octet_ref, rows_ref, between_ref,
        coarse_ref, lanes_ref, out_ref, q_ref, p_ref, x_ref, o_ref, l_ref, z_ref, fold_ref, peak_ref,
    ):
        step = pl.program_id(0)

        @pl.when(step == 0)
        def _():
            out_ref[...] = jnp.zeros_like(out_ref)

        @pl.when(step < plan_ref[slots])
        def _():
            slot = plan_ref[step]
            core = plan_ref[slots + 1]
            base = slot * (BINS + 1)
            first_edge = edge_ref[base]
            last_edge = edge_ref[base + BINS]

            held = strain_ref.shape[3]
            piece = min(held, 16)

            def strain_rows(part, r):
                pieces = []
                for i in range(16 // piece):
                    row = r + i * piece
                    owner = row // held
                    which = (owner + core) % 2
                    inner = pl.multiple_of(row % held, piece)
                    pieces.append(strain_ref[owner // 2, which, part, pl.ds(inner, piece), :])
                return pieces[0] if len(pieces) == 1 else jnp.concatenate(pieces, axis=0)

            def product(r):
                data_r = strain_rows(0, r)
                data_i = strain_rows(1, r)
                wave_r = wave_ref[0, 0, pl.ds(r, 16), :].astype(jnp.float32)
                wave_i = wave_ref[0, 1, pl.ds(r, 16), :].astype(jnp.float32)
                index = (
                    lax.broadcasted_iota(jnp.int32, (16, ROWS), 0) * ROWS
                    + lax.broadcasted_iota(jnp.int32, (16, ROWS), 1)
                    + r * ROWS
                )
                inside = (index >= first_edge) & (index < last_edge)
                real = jnp.where(inside, data_r * wave_r + data_i * wave_i, 0.0)
                imag = jnp.where(inside, data_i * wave_r - data_r * wave_i, 0.0)
                q_ref[0, pl.ds(r, 16), :] = real
                q_ref[1, pl.ds(r, 16), :] = imag
                p_ref[pl.ds(r, 16), :] = wave_r * wave_r + wave_i * wave_i
                return real, imag

            def front(c, carry):
                r = pl.multiple_of(c * 16, 16)
                low_r, low_i = product(r)
                high_r, high_i = product(pl.multiple_of(r + HALF, 16))
                mixed = [
                    (low_r + high_r, low_i + high_i),
                    (low_r - high_i, low_i + high_r),
                    (low_r - high_r, low_i - high_i),
                    (low_r + high_i, low_i - high_r),
                ]
                for v in range(4):
                    real, imag = mixed[v]
                    if v != 2:
                        at = (0, 1, 0, 2)[v]
                        cosine = jnp.concatenate([rows_ref[at, 0, pl.ds(r, 16), :]] * 4, axis=1)
                        sine = jnp.concatenate([rows_ref[at, 1, pl.ds(r, 16), :]] * 4, axis=1)
                        real, imag = real * cosine - imag * sine, real * sine + imag * cosine
                    for part, value in ((0, real), (1, imag)):
                        high, low = split_bf16(value)
                        column = (2 * v + part) * ROWS
                        x_ref[pl.ds(r, 16), column : column + ROWS] = high
                        x_ref[pl.ds(pl.multiple_of(r + HALF, 16), 16), column : column + ROWS] = low
                return carry

            lax.fori_loop(0, HALF // 16, front, 0)

            offset = lax.broadcasted_iota(jnp.int32, (8, ROWS), 0) * ROWS + lax.broadcasted_iota(
                jnp.int32, (8, ROWS), 1
            )
            powers = []
            for b in range(BINS):
                lower = edge_ref[base + b]
                upper = edge_ref[base + b + 1]

                def gather(i, carry, lower=lower, upper=upper):
                    real, imag, power = carry
                    r = pl.multiple_of(i * 8, 8)
                    start = i * (8 * ROWS)
                    mask = (offset >= lower - start) & (offset < upper - start)
                    real = real + jnp.where(mask, q_ref[0, pl.ds(r, 8), :], 0.0)
                    imag = imag + jnp.where(mask, q_ref[1, pl.ds(r, 8), :], 0.0)
                    power = power + jnp.where(mask, p_ref[pl.ds(r, 8), :], 0.0)
                    return real, imag, power

                zero = jnp.zeros((8, ROWS), jnp.float32)
                real, imag, power = lax.fori_loop(
                    lower // (8 * ROWS), (upper + (8 * ROWS - 1)) // (8 * ROWS), gather, (zero, zero, zero)
                )
                fold_ref[0:8, b * ROWS : (b + 1) * ROWS] = real
                fold_ref[8:16, b * ROWS : (b + 1) * ROWS] = imag
                powers.append(jnp.sum(power, axis=(0, 1), keepdims=True))
            energy = powers[0]
            for b in range(1, BINS):
                energy = energy + powers[b]

            lanes_r = lanes_ref[0, 0:1, :]
            lanes_i = lanes_ref[1, 0:1, :]

            for v in range(4):
                column = v * 2 * ROWS
                whole = jnp.dot(
                    first_ref[...],
                    jnp.concatenate(
                        [x_ref[:, column : column + 2 * ROWS], x_ref[0:HALF, column : column + 2 * ROWS]], axis=0
                    ),
                    preferred_element_type=jnp.float32,
                )
                o_ref[...] = whole
                for chunk in range(QUART // CHUNK):
                    u = chunk * CHUNK
                    cos_r = o_ref[u : u + CHUNK, :ROWS]
                    cos_i = o_ref[u : u + CHUNK, ROWS:]
                    sin_r = o_ref[QUART + u : QUART + u + CHUNK, :ROWS]
                    sin_i = o_ref[QUART + u : QUART + u + CHUNK, ROWS:]
                    for mirror in range(2):
                        if mirror == 0:
                            real, imag = cos_r - sin_i, cos_i + sin_r
                        else:
                            real, imag = cos_r + sin_i, cos_i - sin_r
                        cosine = between_ref[v, mirror, 0, u : u + CHUNK, :]
                        sine = between_ref[v, mirror, 1, u : u + CHUNK, :]
                        real, imag = real * cosine - imag * sine, real * sine + imag * cosine
                        values = lane_butterfly(real, imag, lanes_r, lanes_i)
                        for part in range(4):
                            high, low = split_bf16(values[part])
                            at = ((chunk * 2 + mirror) * 4 + part) * CHUNK
                            l_ref[at : at + CHUNK, :HALF] = high
                            l_ref[at : at + CHUNK, HALF:] = low
                z_ref[...] = jnp.dot(
                    jnp.concatenate([l_ref[...], l_ref[:, :HALF]], axis=1),
                    second_ref[...],
                    preferred_element_type=jnp.float32,
                )
                for chunk in range(QUART // CHUNK):
                    for mirror in range(2):
                        cell = chunk if mirror == 0 else 7 - chunk
                        for parity in range(2):
                            at = ((chunk * 2 + mirror) * 4 + parity * 2) * CHUNK
                            real = z_ref[at : at + CHUNK, :]
                            imag = z_ref[at + CHUNK : at + 2 * CHUNK, :]
                            a, d = real[:, :128], real[:, 128:]
                            c, e = imag[:, :128], imag[:, 128:]
                            for side in range(2):
                                if side == 0:
                                    re, im = a - e, c + d
                                else:
                                    re, im = a + e, c - d
                                square = re * re + im * im
                                best = jnp.max(square.reshape(CHUNK // 8, 8, 128), axis=0)
                                lane = (parity * 2 + side) * 128
                                if v:
                                    best = jnp.maximum(best, peak_ref[cell, :, lane : lane + 128])
                                peak_ref[cell, :, lane : lane + 128] = best

            high, low = split_bf16(fold_ref[...])
            bands = jnp.dot(
                octet_ref[...], jnp.concatenate([high, low, high], axis=0), preferred_element_type=jnp.float32
            )
            parts = [[], [], [], []]
            coarse_r = coarse_ref[0]
            coarse_i = coarse_ref[1]
            for b in range(BINS):
                real = bands[0:8, b * ROWS : (b + 1) * ROWS]
                imag = bands[8:16, b * ROWS : (b + 1) * ROWS]
                real, imag = real * coarse_r - imag * coarse_i, real * coarse_i + imag * coarse_r
                values = lane_butterfly(real, imag, lanes_r, lanes_i)
                for part in range(4):
                    parts[part].append(values[part])
            left = jnp.concatenate([value for part in parts for value in part], axis=0)
            high, low = split_bf16(left)
            result = split_dot(high, low, second_ref)
            loud = jnp.concatenate(
                [jnp.max(peak_ref[cell], axis=0, keepdims=True) for cell in range(8)], axis=0
            )
            inverse = 1.0 / energy
            top = jnp.zeros((8, 128), jnp.float32)
            for parity in range(2):
                real = result[parity * 256 : parity * 256 + 128, :]
                imag = result[parity * 256 + 128 : parity * 256 + 256, :]
                a, d = real[:, :128], real[:, 128:]
                c, e = imag[:, :128], imag[:, 128:]
                for side in range(2):
                    if side == 0:
                        re, im = a - e, c + d
                    else:
                        re, im = a + e, c - d
                    re = re.reshape(BINS, 8, 128)
                    im = im.reshape(BINS, 8, 128)
                    total_r = jnp.sum(re, axis=0)
                    total_i = jnp.sum(im, axis=0)
                    misfit = jnp.zeros((8, 128), jnp.float32)
                    for b in range(BINS):
                        weight = powers[b] * inverse
                        error_r = re[b] - weight * total_r
                        error_i = im[b] - weight * total_i
                        misfit = misfit + (error_r * error_r + error_i * error_i) * (1.0 / (powers[b] + EPSILON))
                    reduced = misfit / (2 * BINS - 2)
                    factor = jnp.where(
                        reduced > 1.0, jnp.exp(jnp.log((1.0 + reduced * reduced * reduced) / 2.0) * (-1.0 / 6.0)), 1.0
                    )
                    lane = (parity * 2 + side) * 128
                    top = jnp.maximum(top, jnp.sqrt(loud[:, lane : lane + 128]) * factor)
            best = jnp.max(top, axis=(0, 1), keepdims=True) / jnp.sqrt(energy)
            out_ref[pl.ds(slot, 1), :] = jnp.broadcast_to(best, (1, 128))

    return kernel


def slot_peaks(plan, edges, strain, waves, interpret=False):
    slots = waves.shape[0]
    tables = [jnp.asarray(table) for table in host_tables()]

    def resident(array):
        return pl.BlockSpec(
            array.shape, lambda i, plan, edges, n=array.ndim: (0,) * n, pipeline_mode=pl.Buffered(1)
        )

    return pl.pallas_call(
        make_kernel(slots),
        out_shape=jax.ShapeDtypeStruct((slots, 128), jnp.float32),
        grid_spec=pltpu.PrefetchScalarGridSpec(
            num_scalar_prefetch=2,
            grid=(slots,),
            in_specs=[
                resident(strain),
                pl.BlockSpec((1, 2, ROWS, ROWS), lambda i, plan, edges: (plan[i], 0, 0, 0)),
            ]
            + [resident(table) for table in tables],
            out_specs=pl.BlockSpec((slots, 128), lambda i, plan, edges: (0, 0)),
            scratch_shapes=[
                pltpu.VMEM((2, ROWS, ROWS), jnp.float32),
                pltpu.VMEM((ROWS, ROWS), jnp.float32),
                pltpu.VMEM((ROWS, 8 * ROWS), jnp.bfloat16),
                pltpu.VMEM((HALF, 2 * ROWS), jnp.float32),
                pltpu.VMEM((1024, ROWS), jnp.bfloat16),
                pltpu.VMEM((1024, HALF), jnp.float32),
                pltpu.VMEM((16, BINS * ROWS), jnp.float32),
                pltpu.VMEM((8, 8, ROWS), jnp.float32),
            ],
        ),
        compiler_params=pltpu.CompilerParams(vmem_limit_bytes=48 << 20),
        interpret=interpret,
    )(plan, edges, strain, waves, *tables)


def per_device(strain, templates, counts, edges):
    devices = lax.axis_size("bank")
    device = lax.axis_index("bank")
    core = device % 2
    slots = templates.shape[0]
    mates = [(i, i ^ 1) for i in range(devices)]
    cores = [list(range(c, devices, 2)) for c in range(2)]

    shard = strain.reshape(2, 2, -1, ROWS)
    own = lax.dynamic_index_in_dim(shard, core, 0, keepdims=False)
    other = lax.dynamic_index_in_dim(shard, 1 - core, 0, keepdims=False)
    shard = jnp.stack([own, lax.ppermute(other, "bank", mates)])
    spectrum = lax.all_gather(shard, "bank", axis=0, tiled=False, axis_index_groups=cores)

    small = jnp.concatenate([counts, edges.reshape(-1)])
    mate_small = lax.ppermute(small, "bank", mates)
    mate_waves = lax.ppermute(templates, "bank", mates)
    waves = jnp.concatenate([templates, mate_waves]).reshape(2 * slots, 2, ROWS, ROWS)
    own_count = small[0]
    live = own_count + mate_small[0]
    ramp = jnp.minimum(jnp.arange(2 * slots, dtype=jnp.int32), live - 1)
    order = jnp.where(ramp < own_count, ramp, slots + ramp - own_count)
    plan = jnp.concatenate([order, live[None], core[None]]).astype(jnp.int32)
    all_edges = jnp.concatenate([small[1:], mate_small[1:]])
    peaks = slot_peaks(plan, all_edges, spectrum, waves)[:, 0]

    mine = peaks[:slots]
    theirs = lax.ppermute(peaks[slots:], "bank", mates)
    slot_peak = jnp.where(core == 0, jnp.stack([mine, theirs], axis=1), jnp.stack([theirs, mine], axis=1))
    segment_peak = lax.pmax(jnp.max(slot_peak, axis=0), "bank")
    return (slot_peak, segment_peak)


def solution(mesh):
    placed = (P("seg", None, "bank"), P("bank", None, None), P("bank"), P("bank", None))
    return jax.shard_map(
        per_device,
        mesh=mesh,
        in_specs=placed,
        out_specs=(P("bank", "seg"), P("seg")),
        check_vma=False,
    )
```

```python
import numpy as np

import jax
import jax.numpy as jnp
from jax import lax
from jax.experimental import pallas as pl
from jax.experimental.pallas import tpu as pltpu
from jax.sharding import PartitionSpec as P

CELL = 128
BINS = 16
EPSILON = 1e-06
ROWS = 512
HALF = 256
QUART = 128
CHUNK = 32


def split_bf16(x):
    high = x.astype(jnp.bfloat16)
    low = (x - high.astype(jnp.float32)).astype(jnp.bfloat16)
    return high, low


def host_split(x):
    high = x.astype(np.float32).astype(jnp.bfloat16)
    low = (x - high.astype(np.float64)).astype(np.float32).astype(jnp.bfloat16)
    return high, low


def host_tables():
    k = np.arange(HALF)
    u = np.arange(QUART) + 0.5
    angle = 2 * np.pi * u[:, None] * k[None, :] / HALF
    wave = np.concatenate([np.cos(angle), np.sin(angle)], axis=0)
    high, low = host_split(wave)
    first = np.concatenate([high, high, low], axis=1)
    second = np.concatenate([high.T, high.T, low.T], axis=0)
    eight = 2 * np.pi * (np.arange(8)[:, None] * np.arange(8)[None, :] % 8) / 8
    block = np.block([[np.cos(eight), -np.sin(eight)], [np.sin(eight), np.cos(eight)]])
    high, low = host_split(block)
    octet = np.concatenate([high, high, low], axis=1)
    angle = 2 * np.pi * k[None, :] * np.array([1, 2])[:, None] / 1024
    rows = np.stack([np.cos(angle), np.sin(angle)], axis=1)
    rows = np.broadcast_to(rows[..., None], rows.shape + (128,)).astype(np.float32)
    unit = 2 * np.pi / (1 << 19)
    angle = unit * (4 * np.arange(QUART)[:, None] * np.arange(ROWS))
    between = np.stack([np.cos(angle), np.sin(angle)]).astype(np.float32)
    angle = unit * (np.array([0, 1, 2, 3, 1020, 1021, 1022, 1023])[:, None] * np.arange(ROWS))
    shift = np.stack([np.cos(angle), np.sin(angle)]).astype(np.float32)
    angle = unit * (128 * np.arange(8)[:, None] * np.arange(ROWS)[None, :])
    coarse = np.stack([np.cos(angle), np.sin(angle)]).astype(np.float32)
    angle = -2 * np.pi * k / ROWS
    lanes = np.stack([np.cos(angle), np.sin(angle)]).astype(np.float32)
    lanes = np.broadcast_to(lanes[:, None, :], (2, 8, HALF)).copy()
    return first, second, octet, rows.copy(), between, shift, coarse, lanes


def lane_butterfly(real, imag, lanes_real, lanes_imag):
    low_r, high_r = real[:, :HALF], real[:, HALF:]
    low_i, high_i = imag[:, :HALF], imag[:, HALF:]
    sum_r, sum_i = low_r + high_r, low_i + high_i
    even_r = sum_r * lanes_real - sum_i * lanes_imag
    even_i = sum_r * lanes_imag + sum_i * lanes_real
    return even_r, even_i, low_r - high_r, low_i - high_i


def split_dot(high, low, second_ref):
    return jnp.dot(
        jnp.concatenate([high, low, high], axis=1), second_ref[...], preferred_element_type=jnp.float32
    )


def encode_kernel(core_ref, strain_ref, real_ref, imag_ref):
    rows = strain_ref.shape[2]
    for which in range(2):
        segment = core_ref[0] if which == 0 else 1 - core_ref[0]
        data = [strain_ref[segment, 0], strain_ref[segment, 1]]
        largest = jnp.max(jnp.maximum(jnp.abs(data[0]), jnp.abs(data[1])), axis=1, keepdims=True)
        exponent = jnp.floor(jnp.log2(jnp.maximum(largest, 1e-30)) + 1.001)
        scale = jnp.exp2(15.0 - exponent)
        for value, out_ref in zip(data, (real_ref, imag_ref)):
            number = jnp.clip(jnp.round(value * scale), -32767.0, 32767.0).astype(jnp.int32)
            packed = (number[:, :HALF] << 16) | (number[:, HALF:] & 0xFFFF)
            out_ref[which, 0:rows, :] = packed[:, :128]
            out_ref[which, rows : 2 * rows, :] = packed[:, 128:]
        spread = jnp.broadcast_to(exponent.astype(jnp.int32), (rows, 128))
        same = lax.broadcasted_iota(jnp.int32, (rows, 128), 0) == lax.broadcasted_iota(jnp.int32, (rows, 128), 1)
        line = jnp.sum(jnp.where(same, spread, 0), axis=0, keepdims=True)
        real_ref[which, 2 * rows :, :] = jnp.broadcast_to(line, (8, 128))


def encode(core, strain):
    rows = strain.shape[2]
    return pl.pallas_call(
        encode_kernel,
        out_shape=(
            jax.ShapeDtypeStruct((2, 2 * rows + 8, 128), jnp.int32),
            jax.ShapeDtypeStruct((2, 2 * rows, 128), jnp.int32),
        ),
        in_specs=[pl.BlockSpec(memory_space=pltpu.SMEM), pl.BlockSpec(memory_space=pltpu.VMEM)],
        out_specs=(pl.BlockSpec(memory_space=pltpu.VMEM), pl.BlockSpec(memory_space=pltpu.VMEM)),
    )(core.reshape(1), strain)


def make_kernel(slots, real_masks, imag_masks):
    blocks = [len(masks) for masks in (real_masks, imag_masks)]

    def kernel(*refs):
        plan_ref, edge_ref, own_ref, mate_ref = refs[:4]
        real_refs = refs[4 : 4 + blocks[0]]
        imag_refs = refs[4 + blocks[0] : 4 + sum(blocks)]
        (first_ref, second_ref, octet_ref, rows_ref, base_ref, shift_ref, coarse_ref, lanes_ref, out_ref, strain_ref,
         wave_ref, between_ref, q_ref, p_ref, x_ref, o_ref, l_ref, z_ref, fold_ref, peak_ref, sem) = refs[4 + sum(blocks) :]
        live = plan_ref[slots]
        own_count = plan_ref[slots + 1]
        device = plan_ref[slots + 2]

        def fetch(step):
            slot = plan_ref[step]
            buffer = step % 2

            @pl.when(step < own_count)
            def _():
                pltpu.make_async_copy(own_ref.at[slot], wave_ref.at[buffer], sem.at[buffer]).start()

            @pl.when(step >= own_count)
            def _():
                pltpu.make_async_copy(mate_ref.at[slot - slots // 2], wave_ref.at[buffer], sem.at[buffer]).start()

        fetch(0)
        out_ref[...] = jnp.zeros_like(out_ref)

        held = imag_refs[0].shape[1] // 2
        same = lax.broadcasted_iota(jnp.int32, (held, 128), 0) == lax.broadcasted_iota(jnp.int32, (held, 128), 1)
        for part, (part_refs, masks) in enumerate(((real_refs, real_masks), (imag_refs, imag_masks))):
            for ref, group in zip(part_refs, masks):
                for i, mask in enumerate(group):
                    row = pl.multiple_of((device ^ mask) * held, held)
                    if part == 0:
                        line = jnp.broadcast_to(ref[i, 2 * held : 2 * held + 1, :], (held, 128))
                        exponent = jnp.sum(jnp.where(same, line, 0).astype(jnp.float32), axis=1, keepdims=True)
                        scale = jnp.broadcast_to(jnp.exp2(exponent - 15.0), (held, 128))
                        strain_ref[2, pl.ds(row, held), 0:128] = scale
                    scale = strain_ref[2, pl.ds(row, held), 0:128]
                    for tile in range(2):
                        word = ref[i, tile * held : (tile + 1) * held, :]
                        high = (word >> 16).astype(jnp.float32) * scale
                        low = ((word << 16) >> 16).astype(jnp.float32) * scale
                        strain_ref[part, pl.ds(row, held), tile * 128 : tile * 128 + 128] = high
                        strain_ref[part, pl.ds(row, held), HALF + tile * 128 : HALF + tile * 128 + 128] = low

        for v in range(4):
            for mirror in range(2):
                at = mirror * 4 + v
                base_r = base_ref[0]
                base_i = base_ref[1] if mirror == 0 else -base_ref[1]
                shift_r = shift_ref[0, at : at + 1, :]
                shift_i = shift_ref[1, at : at + 1, :]
                between_ref[v, mirror, 0] = base_r * shift_r - base_i * shift_i
                between_ref[v, mirror, 1] = base_r * shift_i + base_i * shift_r

        def one_slot(step, carry):
            slot = plan_ref[step]
            buffer = step % 2
            base = slot * (BINS + 1)
            first_edge = edge_ref[base]
            last_edge = edge_ref[base + BINS]

            @pl.when(step + 1 < live)
            def _():
                fetch(step + 1)

            pltpu.make_async_copy(own_ref.at[0], wave_ref.at[buffer], sem.at[buffer]).wait()

            def product(r):
                data_r = strain_ref[0, pl.ds(r, 16), :]
                data_i = strain_ref[1, pl.ds(r, 16), :]
                wave_r = wave_ref[buffer, 0, pl.ds(r, 16), :].astype(jnp.float32)
                wave_i = wave_ref[buffer, 1, pl.ds(r, 16), :].astype(jnp.float32)
                index = (
                    lax.broadcasted_iota(jnp.int32, (16, ROWS), 0) * ROWS
                    + lax.broadcasted_iota(jnp.int32, (16, ROWS), 1)
                    + r * ROWS
                )
                inside = (index >= first_edge) & (index < last_edge)
                real = jnp.where(inside, data_r * wave_r + data_i * wave_i, 0.0)
                imag = jnp.where(inside, data_i * wave_r - data_r * wave_i, 0.0)
                q_ref[0, pl.ds(r, 16), :] = real
                q_ref[1, pl.ds(r, 16), :] = imag
                p_ref[pl.ds(r, 16), :] = wave_r * wave_r + wave_i * wave_i
                return real, imag

            def front(c, carry):
                r = pl.multiple_of(c * 16, 16)
                low_r, low_i = product(r)
                high_r, high_i = product(pl.multiple_of(r + HALF, 16))
                mixed = [
                    (low_r + high_r, low_i + high_i),
                    (low_r - high_i, low_i + high_r),
                    (low_r - high_r, low_i - high_i),
                    (low_r + high_i, low_i - high_r),
                ]
                for v in range(4):
                    real, imag = mixed[v]
                    if v != 2:
                        at = (1, 0, 0, 0)[v]
                        cosine = jnp.concatenate([rows_ref[at, 0, pl.ds(r, 16), :]] * 4, axis=1)
                        sine = jnp.concatenate([rows_ref[at, 1, pl.ds(r, 16), :]] * 4, axis=1)
                        if v == 3:
                            real, imag = real * cosine - imag * sine, real * sine + imag * cosine
                        else:
                            real, imag = real * cosine + imag * sine, imag * cosine - real * sine
                    for part, value in ((0, real), (1, imag)):
                        high, low = split_bf16(value)
                        column = (2 * v + part) * ROWS
                        x_ref[pl.ds(r, 16), column : column + ROWS] = high
                        x_ref[pl.ds(pl.multiple_of(r + HALF, 16), 16), column : column + ROWS] = low
                return carry

            lax.fori_loop(0, HALF // 16, front, 0)

            offset = lax.broadcasted_iota(jnp.int32, (8, ROWS), 0) * ROWS + lax.broadcasted_iota(
                jnp.int32, (8, ROWS), 1
            )
            powers = []
            for b in range(BINS):
                lower = edge_ref[base + b]
                upper = edge_ref[base + b + 1]

                def gather(i, carry, lower=lower, upper=upper):
                    real, imag, power = carry
                    r = pl.multiple_of(i * 8, 8)
                    start = i * (8 * ROWS)
                    mask = (offset >= lower - start) & (offset < upper - start)
                    real = real + jnp.where(mask, q_ref[0, pl.ds(r, 8), :], 0.0)
                    imag = imag + jnp.where(mask, q_ref[1, pl.ds(r, 8), :], 0.0)
                    power = power + jnp.where(mask, p_ref[pl.ds(r, 8), :], 0.0)
                    return real, imag, power

                zero = jnp.zeros((8, ROWS), jnp.float32)
                real, imag, power = lax.fori_loop(
                    lower // (8 * ROWS), (upper + (8 * ROWS - 1)) // (8 * ROWS), gather, (zero, zero, zero)
                )
                fold_ref[0:8, b * ROWS : (b + 1) * ROWS] = real
                fold_ref[8:16, b * ROWS : (b + 1) * ROWS] = imag
                powers.append(jnp.sum(power, axis=(0, 1), keepdims=True))
            energy = powers[0]
            for b in range(1, BINS):
                energy = energy + powers[b]

            lanes_r = lanes_ref[0, 0:1, :]
            lanes_i = lanes_ref[1, 0:1, :]

            for v in range(4):
                column = v * 2 * ROWS
                whole = jnp.dot(
                    first_ref[...],
                    jnp.concatenate(
                        [x_ref[:, column : column + 2 * ROWS], x_ref[0:HALF, column : column + 2 * ROWS]], axis=0
                    ),
                    preferred_element_type=jnp.float32,
                )
                o_ref[...] = whole
                for chunk in range(QUART // CHUNK):
                    u = chunk * CHUNK
                    cos_r = o_ref[u : u + CHUNK, :ROWS]
                    cos_i = o_ref[u : u + CHUNK, ROWS:]
                    sin_r = o_ref[QUART + u : QUART + u + CHUNK, :ROWS]
                    sin_i = o_ref[QUART + u : QUART + u + CHUNK, ROWS:]
                    for mirror in range(2):
                        if mirror == 0:
                            real, imag = cos_r - sin_i, cos_i + sin_r
                        else:
                            real, imag = cos_r + sin_i, cos_i - sin_r
                        cosine = between_ref[v, mirror, 0, u : u + CHUNK, :]
                        sine = between_ref[v, mirror, 1, u : u + CHUNK, :]
                        real, imag = real * cosine - imag * sine, real * sine + imag * cosine
                        values = lane_butterfly(real, imag, lanes_r, lanes_i)
                        for part in range(4):
                            high, low = split_bf16(values[part])
                            at = ((chunk * 2 + mirror) * 4 + part) * CHUNK
                            l_ref[at : at + CHUNK, :HALF] = high
                            l_ref[at : at + CHUNK, HALF:] = low
                z_ref[...] = jnp.dot(
                    jnp.concatenate([l_ref[...], l_ref[:, :HALF]], axis=1),
                    second_ref[...],
                    preferred_element_type=jnp.float32,
                )
                for chunk in range(QUART // CHUNK):
                    for mirror in range(2):
                        cell = chunk if mirror == 0 else 7 - chunk
                        for parity in range(2):
                            at = ((chunk * 2 + mirror) * 4 + parity * 2) * CHUNK
                            real = z_ref[at : at + CHUNK, :]
                            imag = z_ref[at + CHUNK : at + 2 * CHUNK, :]
                            a, d = real[:, :128], real[:, 128:]
                            c, e = imag[:, :128], imag[:, 128:]
                            for side in range(2):
                                if side == 0:
                                    re, im = a - e, c + d
                                else:
                                    re, im = a + e, c - d
                                square = re * re + im * im
                                best = jnp.max(square.reshape(CHUNK // 8, 8, 128), axis=0)
                                lane = (parity * 2 + side) * 128
                                if v:
                                    best = jnp.maximum(best, peak_ref[cell, :, lane : lane + 128])
                                peak_ref[cell, :, lane : lane + 128] = best

            high, low = split_bf16(fold_ref[...])
            bands = jnp.dot(
                octet_ref[...], jnp.concatenate([high, low, high], axis=0), preferred_element_type=jnp.float32
            )
            parts = [[], [], [], []]
            coarse_r = coarse_ref[0]
            coarse_i = coarse_ref[1]
            for b in range(BINS):
                real = bands[0:8, b * ROWS : (b + 1) * ROWS]
                imag = bands[8:16, b * ROWS : (b + 1) * ROWS]
                real, imag = real * coarse_r - imag * coarse_i, real * coarse_i + imag * coarse_r
                values = lane_butterfly(real, imag, lanes_r, lanes_i)
                for part in range(4):
                    parts[part].append(values[part])
            left = jnp.concatenate([value for part in parts for value in part], axis=0)
            high, low = split_bf16(left)
            result = split_dot(high, low, second_ref)
            loud = jnp.concatenate(
                [jnp.max(peak_ref[cell], axis=0, keepdims=True) for cell in range(8)], axis=0
            )
            inverse = 1.0 / energy
            top = jnp.zeros((8, 128), jnp.float32)
            for parity in range(2):
                real = result[parity * 256 : parity * 256 + 128, :]
                imag = result[parity * 256 + 128 : parity * 256 + 256, :]
                a, d = real[:, :128], real[:, 128:]
                c, e = imag[:, :128], imag[:, 128:]
                for side in range(2):
                    if side == 0:
                        re, im = a - e, c + d
                    else:
                        re, im = a + e, c - d
                    re = re.reshape(BINS, 8, 128)
                    im = im.reshape(BINS, 8, 128)
                    total_r = jnp.sum(re, axis=0)
                    total_i = jnp.sum(im, axis=0)
                    misfit = jnp.zeros((8, 128), jnp.float32)
                    for b in range(BINS):
                        weight = powers[b] * inverse
                        error_r = re[b] - weight * total_r
                        error_i = im[b] - weight * total_i
                        misfit = misfit + (error_r * error_r + error_i * error_i) * (1.0 / (powers[b] + EPSILON))
                    reduced = misfit / (2 * BINS - 2)
                    factor = jnp.where(
                        reduced > 1.0, jnp.exp(jnp.log((1.0 + reduced * reduced * reduced) / 2.0) * (-1.0 / 6.0)), 1.0
                    )
                    lane = (parity * 2 + side) * 128
                    top = jnp.maximum(top, jnp.sqrt(loud[:, lane : lane + 128]) * factor)
            best = jnp.max(top, axis=(0, 1), keepdims=True) / jnp.sqrt(energy)
            out_ref[pl.ds(slot, 1), :] = jnp.broadcast_to(best, (1, 128))
            return carry

        lax.fori_loop(0, live, one_slot, 0)

    return kernel


def slot_peaks(plan, edges, own_waves, mate_waves, real_blocks, imag_blocks, real_masks, imag_masks):
    slots = 2 * own_waves.shape[0]
    tables = [jnp.asarray(table) for table in host_tables()]
    smem = pl.BlockSpec(memory_space=pltpu.SMEM)
    hbm = pl.BlockSpec(memory_space=pl.ANY)
    vmem = pl.BlockSpec(memory_space=pltpu.VMEM)
    return pl.pallas_call(
        make_kernel(slots, real_masks, imag_masks),
        out_shape=jax.ShapeDtypeStruct((slots, 128), jnp.float32),
        in_specs=[smem, smem, hbm, hbm] + [vmem] * (len(real_blocks) + len(imag_blocks) + len(tables)),
        out_specs=vmem,
        scratch_shapes=[
            pltpu.VMEM((3, ROWS, ROWS), jnp.float32),
            pltpu.VMEM((2, 2, ROWS, ROWS), jnp.bfloat16),
            pltpu.VMEM((4, 2, 2, QUART, ROWS), jnp.float32),
            pltpu.VMEM((2, ROWS, ROWS), jnp.float32),
            pltpu.VMEM((ROWS, ROWS), jnp.float32),
            pltpu.VMEM((ROWS, 8 * ROWS), jnp.bfloat16),
            pltpu.VMEM((HALF, 2 * ROWS), jnp.float32),
            pltpu.VMEM((1024, ROWS), jnp.bfloat16),
            pltpu.VMEM((1024, HALF), jnp.float32),
            pltpu.VMEM((16, BINS * ROWS), jnp.float32),
            pltpu.VMEM((8, 8, ROWS), jnp.float32),
            pltpu.SemaphoreType.DMA((2,)),
        ],
        compiler_params=pltpu.CompilerParams(vmem_limit_bytes=48 << 20),
    )(plan, edges, own_waves, mate_waves, *real_blocks, *imag_blocks, *tables)


def exchange(x, bit):
    devices = lax.axis_size("bank")
    return lax.ppermute(x, "bank", [(i, i ^ bit) for i in range(devices)])


def per_device(strain, templates, counts, edges):
    devices = lax.axis_size("bank")
    device = lax.axis_index("bank").astype(jnp.int32)
    core = device % 2
    slots = templates.shape[0]
    bits = [1 << i for i in range(1, devices.bit_length() - 1)]
    orders = [bits[::-1], bits[:1] + bits[:0:-1]]

    coded = encode(core, strain.reshape(2, 2, -1, ROWS))
    current = [jnp.stack([part[0], exchange(part[1], 1)]) for part in coded]
    masks = [[0, 1], [0, 1]]
    for level in range(len(bits)):
        arrived = [exchange(current[half], orders[half][level]) for half in range(2)]
        added = [[m ^ orders[half][level] for m in masks[half]] for half in range(2)]
        if level + 1 < len(bits):
            current = [jnp.concatenate([current[half], arrived[half]]) for half in range(2)]
            masks = [masks[half] + added[half] for half in range(2)]
    blocks = [[current[half], arrived[half]] for half in range(2)]
    block_masks = [[masks[half], added[half]] for half in range(2)]

    small = jnp.concatenate([counts, edges.reshape(-1)])
    mate_small = exchange(small, 1)
    own_waves = templates.reshape(slots, 2, ROWS, ROWS)
    mate_waves = exchange(own_waves, 1)
    own_count = small[0]
    live = own_count + mate_small[0]
    ramp = jnp.minimum(jnp.arange(2 * slots, dtype=jnp.int32), live - 1)
    order = jnp.where(ramp < own_count, ramp, slots + ramp - own_count)
    plan = jnp.concatenate([order, live[None], own_count[None], device[None]]).astype(jnp.int32)
    all_edges = jnp.concatenate([small[1:], mate_small[1:]])
    peaks = slot_peaks(plan, all_edges, own_waves, mate_waves, *blocks, *block_masks)[:, 0]

    mine = peaks[:slots]
    here = jnp.max(peaks)
    theirs = exchange(jnp.concatenate([peaks[slots:], here[None]]), 1)
    there = theirs[slots]
    theirs = theirs[:slots]
    slot_peak = jnp.where(core == 0, jnp.stack([mine, theirs], axis=1), jnp.stack([theirs, mine], axis=1))
    segment_peak = jnp.where(core == 0, jnp.stack([here, there]), jnp.stack([there, here]))
    for bit in bits:
        segment_peak = jnp.maximum(segment_peak, exchange(segment_peak, bit))
    return (slot_peak, segment_peak)


def solution(mesh):
    placed = (P("seg", None, "bank"), P("bank", None, None), P("bank"), P("bank", None))
    return jax.shard_map(
        per_device,
        mesh=mesh,
        in_specs=placed,
        out_specs=(P("bank", "seg"), P("seg")),
        check_vma=False,
    )
```

```python
import numpy as np

import jax
import jax.numpy as jnp
from jax import lax
from jax.experimental import pallas as pl
from jax.experimental.pallas import tpu as pltpu
from jax.sharding import PartitionSpec as P

CELL = 128
BINS = 16
EPSILON = 1e-06
ROWS = 512
HALF = 256
QUART = 128
CHUNK = 32


def split_bf16(x):
    high = x.astype(jnp.bfloat16)
    low = (x - high.astype(jnp.float32)).astype(jnp.bfloat16)
    return high, low


def host_split(x):
    high = x.astype(np.float32).astype(jnp.bfloat16)
    low = (x - high.astype(np.float64)).astype(np.float32).astype(jnp.bfloat16)
    return high, low


def host_tables():
    k = np.arange(HALF)
    u = np.arange(QUART) + 0.5
    angle = 2 * np.pi * u[:, None] * k[None, :] / HALF
    wave = np.concatenate([np.cos(angle), np.sin(angle)], axis=0)
    high, low = host_split(wave)
    first = np.concatenate([high, high, low], axis=1)
    second = np.concatenate([high.T, high.T, low.T], axis=0)
    eight = 2 * np.pi * (np.arange(8)[:, None] * np.arange(8)[None, :] % 8) / 8
    block = np.block([[np.cos(eight), -np.sin(eight)], [np.sin(eight), np.cos(eight)]])
    high, low = host_split(block)
    octet = np.concatenate([high, high, low], axis=1)
    angle = 2 * np.pi * k[None, :] * np.array([1, 2])[:, None] / 1024
    rows = np.stack([np.cos(angle), np.sin(angle)], axis=1)
    rows = np.broadcast_to(rows[..., None], rows.shape + (128,)).astype(np.float32)
    unit = 2 * np.pi / (1 << 19)
    angle = unit * (4 * np.arange(QUART)[:, None] * np.arange(ROWS))
    between = np.stack([np.cos(angle), np.sin(angle)]).astype(np.float32)
    angle = unit * (np.array([0, 1, 2, 3, 1020, 1021, 1022, 1023])[:, None] * np.arange(ROWS))
    shift = np.stack([np.cos(angle), np.sin(angle)]).astype(np.float32)
    angle = unit * (128 * np.arange(8)[:, None] * np.arange(ROWS)[None, :])
    coarse = np.stack([np.cos(angle), np.sin(angle)]).astype(np.float32)
    angle = -2 * np.pi * k / ROWS
    lanes = np.stack([np.cos(angle), np.sin(angle)]).astype(np.float32)
    lanes = np.broadcast_to(lanes[:, None, :], (2, 8, HALF)).copy()
    return first, second, octet, rows.copy(), between, shift, coarse, lanes


def lane_butterfly(real, imag, lanes_real, lanes_imag):
    low_r, high_r = real[:, :HALF], real[:, HALF:]
    low_i, high_i = imag[:, :HALF], imag[:, HALF:]
    sum_r, sum_i = low_r + high_r, low_i + high_i
    even_r = sum_r * lanes_real - sum_i * lanes_imag
    even_i = sum_r * lanes_imag + sum_i * lanes_real
    return even_r, even_i, low_r - high_r, low_i - high_i


def split_dot(high, low, second_ref):
    return jnp.dot(
        jnp.concatenate([high, low, high], axis=1), second_ref[...], preferred_element_type=jnp.float32
    )


def encode_kernel(core_ref, strain_ref, real_ref, imag_ref):
    rows = strain_ref.shape[2]
    for which in range(2):
        segment = core_ref[0] if which == 0 else 1 - core_ref[0]
        data = [strain_ref[segment, 0], strain_ref[segment, 1]]
        largest = jnp.max(jnp.maximum(jnp.abs(data[0]), jnp.abs(data[1])), axis=1, keepdims=True)
        exponent = jnp.floor(jnp.log2(jnp.maximum(largest, 1e-30)) + 1.001)
        scale = jnp.exp2(15.0 - exponent)
        for value, out_ref in zip(data, (real_ref, imag_ref)):
            number = jnp.clip(jnp.round(value * scale), -32767.0, 32767.0).astype(jnp.int32)
            packed = (number[:, :HALF] << 16) | (number[:, HALF:] & 0xFFFF)
            out_ref[which, 0:rows, :] = packed[:, :128]
            out_ref[which, rows : 2 * rows, :] = packed[:, 128:]
        spread = jnp.broadcast_to(exponent.astype(jnp.int32), (rows, 128))
        same = lax.broadcasted_iota(jnp.int32, (rows, 128), 0) == lax.broadcasted_iota(jnp.int32, (rows, 128), 1)
        line = jnp.sum(jnp.where(same, spread, 0), axis=0, keepdims=True)
        real_ref[which, 2 * rows :, :] = jnp.broadcast_to(line, (8, 128))


def encode(core, strain):
    rows = strain.shape[2]
    return pl.pallas_call(
        encode_kernel,
        out_shape=(
            jax.ShapeDtypeStruct((2, 2 * rows + 8, 128), jnp.int32),
            jax.ShapeDtypeStruct((2, 2 * rows, 128), jnp.int32),
        ),
        in_specs=[pl.BlockSpec(memory_space=pltpu.SMEM), pl.BlockSpec(memory_space=pltpu.VMEM)],
        out_specs=(pl.BlockSpec(memory_space=pltpu.VMEM), pl.BlockSpec(memory_space=pltpu.VMEM)),
    )(core.reshape(1), strain)


def make_kernel(slots, real_masks, imag_masks):
    blocks = [len(masks) for masks in (real_masks, imag_masks)]

    def kernel(*refs):
        plan_ref, edge_ref, own_ref, mate_ref = refs[:4]
        real_refs = refs[4 : 4 + blocks[0]]
        imag_refs = refs[4 + blocks[0] : 4 + sum(blocks)]
        (first_ref, second_ref, octet_ref, rows_ref, base_ref, shift_ref, coarse_ref, lanes_ref, out_ref, strain_ref,
         wave_ref, between_ref, q_ref, p_ref, x_ref, o_ref, l_ref, z_ref, fold_ref, peak_ref, sem) = refs[4 + sum(blocks) :]
        live = plan_ref[slots]
        own_count = plan_ref[slots + 1]
        device = plan_ref[slots + 2]

        def fetch(step):
            slot = plan_ref[step]
            buffer = step % 2

            @pl.when(step < own_count)
            def _():
                pltpu.make_async_copy(own_ref.at[slot], wave_ref.at[buffer], sem.at[buffer]).start()

            @pl.when(step >= own_count)
            def _():
                pltpu.make_async_copy(mate_ref.at[slot - slots // 2], wave_ref.at[buffer], sem.at[buffer]).start()

        fetch(0)
        out_ref[...] = jnp.zeros_like(out_ref)

        held = imag_refs[0].shape[1] // 2
        same = lax.broadcasted_iota(jnp.int32, (held, 128), 0) == lax.broadcasted_iota(jnp.int32, (held, 128), 1)
        for part, (part_refs, masks) in enumerate(((real_refs, real_masks), (imag_refs, imag_masks))):
            for ref, group in zip(part_refs, masks):
                for i, mask in enumerate(group):
                    row = pl.multiple_of((device ^ mask) * held, held)
                    if part == 0:
                        line = jnp.broadcast_to(ref[i, 2 * held : 2 * held + 1, :], (held, 128))
                        exponent = jnp.sum(jnp.where(same, line, 0).astype(jnp.float32), axis=1, keepdims=True)
                        scale = jnp.broadcast_to(jnp.exp2(exponent - 15.0), (held, 128))
                        strain_ref[2, pl.ds(row, held), 0:128] = scale
                    scale = strain_ref[2, pl.ds(row, held), 0:128]
                    for tile in range(2):
                        word = ref[i, tile * held : (tile + 1) * held, :]
                        high = (word >> 16).astype(jnp.float32) * scale
                        low = ((word << 16) >> 16).astype(jnp.float32) * scale
                        strain_ref[part, pl.ds(row, held), tile * 128 : tile * 128 + 128] = high
                        strain_ref[part, pl.ds(row, held), HALF + tile * 128 : HALF + tile * 128 + 128] = low

        for v in range(4):
            for mirror in range(2):
                at = mirror * 4 + v
                base_r = base_ref[0]
                base_i = base_ref[1] if mirror == 0 else -base_ref[1]
                shift_r = shift_ref[0, at : at + 1, :]
                shift_i = shift_ref[1, at : at + 1, :]
                between_ref[v, mirror, 0] = base_r * shift_r - base_i * shift_i
                between_ref[v, mirror, 1] = base_r * shift_i + base_i * shift_r

        def one_slot(step, carry):
            slot = plan_ref[step]
            buffer = step % 2
            base = slot * (BINS + 1)
            first_edge = edge_ref[base]
            last_edge = edge_ref[base + BINS]

            @pl.when(step + 1 < live)
            def _():
                fetch(step + 1)

            pltpu.make_async_copy(own_ref.at[0], wave_ref.at[buffer], sem.at[buffer]).wait()

            def product(r):
                data_r = strain_ref[0, pl.ds(r, 16), :]
                data_i = strain_ref[1, pl.ds(r, 16), :]
                wave_r = wave_ref[buffer, 0, pl.ds(r, 16), :].astype(jnp.float32)
                wave_i = wave_ref[buffer, 1, pl.ds(r, 16), :].astype(jnp.float32)
                index = (
                    lax.broadcasted_iota(jnp.int32, (16, ROWS), 0) * ROWS
                    + lax.broadcasted_iota(jnp.int32, (16, ROWS), 1)
                    + r * ROWS
                )
                inside = (index >= first_edge) & (index < last_edge)
                real = jnp.where(inside, data_r * wave_r + data_i * wave_i, 0.0)
                imag = jnp.where(inside, data_i * wave_r - data_r * wave_i, 0.0)
                q_ref[0, pl.ds(r, 16), :] = real
                q_ref[1, pl.ds(r, 16), :] = imag
                p_ref[pl.ds(r, 16), :] = wave_r * wave_r + wave_i * wave_i
                return real, imag

            def front(c, carry):
                r = pl.multiple_of(c * 16, 16)
                low_r, low_i = product(r)
                high_r, high_i = product(pl.multiple_of(r + HALF, 16))
                mixed = [
                    (low_r + high_r, low_i + high_i),
                    (low_r - high_i, low_i + high_r),
                    (low_r - high_r, low_i - high_i),
                    (low_r + high_i, low_i - high_r),
                ]
                for v in range(4):
                    real, imag = mixed[v]
                    if v != 2:
                        at = (1, 0, 0, 0)[v]
                        cosine = jnp.concatenate([rows_ref[at, 0, pl.ds(r, 16), :]] * 4, axis=1)
                        sine = jnp.concatenate([rows_ref[at, 1, pl.ds(r, 16), :]] * 4, axis=1)
                        if v == 3:
                            real, imag = real * cosine - imag * sine, real * sine + imag * cosine
                        else:
                            real, imag = real * cosine + imag * sine, imag * cosine - real * sine
                    for part, value in ((0, real), (1, imag)):
                        high, low = split_bf16(value)
                        column = (2 * v + part) * ROWS
                        x_ref[pl.ds(r, 16), column : column + ROWS] = high
                        x_ref[pl.ds(pl.multiple_of(r + HALF, 16), 16), column : column + ROWS] = low
                return carry

            lax.fori_loop(0, HALF // 16, front, 0)

            offset = lax.broadcasted_iota(jnp.int32, (8, ROWS), 0) * ROWS + lax.broadcasted_iota(
                jnp.int32, (8, ROWS), 1
            )
            powers = []
            for b in range(BINS):
                lower = edge_ref[base + b]
                upper = edge_ref[base + b + 1]

                def gather(i, carry, lower=lower, upper=upper):
                    real, imag, power = carry
                    r = pl.multiple_of(i * 8, 8)
                    start = i * (8 * ROWS)
                    mask = (offset >= lower - start) & (offset < upper - start)
                    real = real + jnp.where(mask, q_ref[0, pl.ds(r, 8), :], 0.0)
                    imag = imag + jnp.where(mask, q_ref[1, pl.ds(r, 8), :], 0.0)
                    power = power + jnp.where(mask, p_ref[pl.ds(r, 8), :], 0.0)
                    return real, imag, power

                zero = jnp.zeros((8, ROWS), jnp.float32)
                real, imag, power = lax.fori_loop(
                    lower // (8 * ROWS), (upper + (8 * ROWS - 1)) // (8 * ROWS), gather, (zero, zero, zero)
                )
                fold_ref[0:8, b * ROWS : (b + 1) * ROWS] = real
                fold_ref[8:16, b * ROWS : (b + 1) * ROWS] = imag
                powers.append(jnp.sum(power, axis=(0, 1), keepdims=True))
            energy = powers[0]
            for b in range(1, BINS):
                energy = energy + powers[b]

            lanes_r = lanes_ref[0, 0:1, :]
            lanes_i = lanes_ref[1, 0:1, :]

            for v in range(4):
                column = v * 2 * ROWS
                whole = jnp.dot(
                    first_ref[...],
                    jnp.concatenate(
                        [x_ref[:, column : column + 2 * ROWS], x_ref[0:HALF, column : column + 2 * ROWS]], axis=0
                    ),
                    preferred_element_type=jnp.float32,
                )
                o_ref[...] = whole
                for chunk in range(QUART // CHUNK):
                    u = chunk * CHUNK
                    cos_r = o_ref[u : u + CHUNK, :ROWS]
                    cos_i = o_ref[u : u + CHUNK, ROWS:]
                    sin_r = o_ref[QUART + u : QUART + u + CHUNK, :ROWS]
                    sin_i = o_ref[QUART + u : QUART + u + CHUNK, ROWS:]
                    for mirror in range(2):
                        if mirror == 0:
                            real, imag = cos_r - sin_i, cos_i + sin_r
                        else:
                            real, imag = cos_r + sin_i, cos_i - sin_r
                        cosine = between_ref[v, mirror, 0, u : u + CHUNK, :]
                        sine = between_ref[v, mirror, 1, u : u + CHUNK, :]
                        real, imag = real * cosine - imag * sine, real * sine + imag * cosine
                        values = lane_butterfly(real, imag, lanes_r, lanes_i)
                        for part in range(4):
                            high, low = split_bf16(values[part])
                            at = ((chunk * 2 + mirror) * 4 + part) * CHUNK
                            l_ref[at : at + CHUNK, :HALF] = high
                            l_ref[at : at + CHUNK, HALF:] = low
                z_ref[...] = jnp.dot(
                    jnp.concatenate([l_ref[...], l_ref[:, :HALF]], axis=1),
                    second_ref[...],
                    preferred_element_type=jnp.float32,
                )
                for chunk in range(QUART // CHUNK):
                    for mirror in range(2):
                        cell = chunk if mirror == 0 else 7 - chunk
                        for parity in range(2):
                            at = ((chunk * 2 + mirror) * 4 + parity * 2) * CHUNK
                            real = z_ref[at : at + CHUNK, :]
                            imag = z_ref[at + CHUNK : at + 2 * CHUNK, :]
                            a, d = real[:, :128], real[:, 128:]
                            c, e = imag[:, :128], imag[:, 128:]
                            for side in range(2):
                                if side == 0:
                                    re, im = a - e, c + d
                                else:
                                    re, im = a + e, c - d
                                square = re * re + im * im
                                best = jnp.max(square.reshape(CHUNK // 8, 8, 128), axis=0)
                                lane = (parity * 2 + side) * 128
                                if v:
                                    best = jnp.maximum(best, peak_ref[cell, :, lane : lane + 128])
                                peak_ref[cell, :, lane : lane + 128] = best

            high, low = split_bf16(fold_ref[...])
            bands = jnp.dot(
                octet_ref[...], jnp.concatenate([high, low, high], axis=0), preferred_element_type=jnp.float32
            )
            parts = [[], [], [], []]
            coarse_r = coarse_ref[0]
            coarse_i = coarse_ref[1]
            for b in range(BINS):
                real = bands[0:8, b * ROWS : (b + 1) * ROWS]
                imag = bands[8:16, b * ROWS : (b + 1) * ROWS]
                real, imag = real * coarse_r - imag * coarse_i, real * coarse_i + imag * coarse_r
                values = lane_butterfly(real, imag, lanes_r, lanes_i)
                for part in range(4):
                    parts[part].append(values[part])
            left = jnp.concatenate([value for part in parts for value in part], axis=0)
            high, low = split_bf16(left)
            result = split_dot(high, low, second_ref)
            loud = jnp.concatenate(
                [jnp.max(peak_ref[cell], axis=0, keepdims=True) for cell in range(8)], axis=0
            )
            inverse = 1.0 / energy
            top = jnp.zeros((8, 128), jnp.float32)
            for parity in range(2):
                real = result[parity * 256 : parity * 256 + 128, :]
                imag = result[parity * 256 + 128 : parity * 256 + 256, :]
                a, d = real[:, :128], real[:, 128:]
                c, e = imag[:, :128], imag[:, 128:]
                for side in range(2):
                    if side == 0:
                        re, im = a - e, c + d
                    else:
                        re, im = a + e, c - d
                    re = re.reshape(BINS, 8, 128)
                    im = im.reshape(BINS, 8, 128)
                    total_r = jnp.sum(re, axis=0)
                    total_i = jnp.sum(im, axis=0)
                    misfit = jnp.zeros((8, 128), jnp.float32)
                    for b in range(BINS):
                        weight = powers[b] * inverse
                        error_r = re[b] - weight * total_r
                        error_i = im[b] - weight * total_i
                        misfit = misfit + (error_r * error_r + error_i * error_i) * (1.0 / (powers[b] + EPSILON))
                    reduced = misfit / (2 * BINS - 2)
                    factor = jnp.where(
                        reduced > 1.0, jnp.exp(jnp.log((1.0 + reduced * reduced * reduced) / 2.0) * (-1.0 / 6.0)), 1.0
                    )
                    lane = (parity * 2 + side) * 128
                    top = jnp.maximum(top, jnp.sqrt(loud[:, lane : lane + 128]) * factor)
            best = jnp.max(top, axis=(0, 1), keepdims=True) / jnp.sqrt(energy)
            out_ref[pl.ds(slot, 1), :] = jnp.broadcast_to(best, (1, 128))
            return carry

        lax.fori_loop(0, live, one_slot, 0)

    return kernel


def slot_peaks(plan, edges, own_waves, mate_waves, real_blocks, imag_blocks, real_masks, imag_masks):
    slots = 2 * own_waves.shape[0]
    tables = [jnp.asarray(table) for table in host_tables()]
    smem = pl.BlockSpec(memory_space=pltpu.SMEM)
    hbm = pl.BlockSpec(memory_space=pl.ANY)
    vmem = pl.BlockSpec(memory_space=pltpu.VMEM)
    return pl.pallas_call(
        make_kernel(slots, real_masks, imag_masks),
        out_shape=jax.ShapeDtypeStruct((slots, 128), jnp.float32),
        in_specs=[smem, smem, hbm, hbm] + [vmem] * (len(real_blocks) + len(imag_blocks) + len(tables)),
        out_specs=vmem,
        scratch_shapes=[
            pltpu.VMEM((3, ROWS, ROWS), jnp.float32),
            pltpu.VMEM((2, 2, ROWS, ROWS), jnp.bfloat16),
            pltpu.VMEM((4, 2, 2, QUART, ROWS), jnp.float32),
            pltpu.VMEM((2, ROWS, ROWS), jnp.float32),
            pltpu.VMEM((ROWS, ROWS), jnp.float32),
            pltpu.VMEM((ROWS, 8 * ROWS), jnp.bfloat16),
            pltpu.VMEM((HALF, 2 * ROWS), jnp.float32),
            pltpu.VMEM((1024, ROWS), jnp.bfloat16),
            pltpu.VMEM((1024, HALF), jnp.float32),
            pltpu.VMEM((16, BINS * ROWS), jnp.float32),
            pltpu.VMEM((8, 8, ROWS), jnp.float32),
            pltpu.SemaphoreType.DMA((2,)),
        ],
        compiler_params=pltpu.CompilerParams(vmem_limit_bytes=48 << 20),
    )(plan, edges, own_waves, mate_waves, *real_blocks, *imag_blocks, *tables)


def exchange(x, bit):
    devices = lax.axis_size("bank")
    return lax.ppermute(x, "bank", [(i, i ^ bit) for i in range(devices)])


def per_device(strain, templates, counts, edges):
    devices = lax.axis_size("bank")
    device = lax.axis_index("bank").astype(jnp.int32)
    core = device % 2
    slots = templates.shape[0]
    bits = [1 << i for i in range(1, devices.bit_length() - 1)]
    orders = [bits[::-1], bits[:1] + bits[:0:-1]]

    coded = encode(core, strain.reshape(2, 2, -1, ROWS))
    current = [jnp.stack([part[0], exchange(part[1], 1)]) for part in coded]
    templates, *current = lax.optimization_barrier((templates, *current))
    masks = [[0, 1], [0, 1]]
    for level in range(len(bits)):
        arrived = [exchange(current[half], orders[half][level]) for half in range(2)]
        added = [[m ^ orders[half][level] for m in masks[half]] for half in range(2)]
        if level + 1 < len(bits):
            current = [jnp.concatenate([current[half], arrived[half]]) for half in range(2)]
            masks = [masks[half] + added[half] for half in range(2)]
    blocks = [[current[half], arrived[half]] for half in range(2)]
    block_masks = [[masks[half], added[half]] for half in range(2)]

    small = jnp.concatenate([counts, edges.reshape(-1)])
    mate_small = exchange(small, 1)
    own_waves = templates.reshape(slots, 2, ROWS, ROWS)
    mate_waves = exchange(own_waves, 1)
    own_count = small[0]
    live = own_count + mate_small[0]
    ramp = jnp.minimum(jnp.arange(2 * slots, dtype=jnp.int32), live - 1)
    order = jnp.where(ramp < own_count, ramp, slots + ramp - own_count)
    plan = jnp.concatenate([order, live[None], own_count[None], device[None]]).astype(jnp.int32)
    all_edges = jnp.concatenate([small[1:], mate_small[1:]])
    peaks = slot_peaks(plan, all_edges, own_waves, mate_waves, *blocks, *block_masks)

    mine = lax.broadcasted_iota(jnp.int32, peaks.shape, 1) % 2 == core
    arrived = exchange(peaks, 1)
    swapped = jnp.concatenate([arrived[slots:], arrived[:slots]])
    both = jnp.where(mine, peaks, swapped)
    best = both
    for bit in bits:
        best = jnp.maximum(best, exchange(best, bit))
    return (both[:slots, :2], jnp.max(best, axis=0)[:2])


def solution(mesh):
    placed = (P("seg", None, "bank"), P("bank", None, None), P("bank"), P("bank", None))
    return jax.shard_map(
        per_device,
        mesh=mesh,
        in_specs=placed,
        out_specs=(P("bank", "seg"), P("seg")),
        check_vma=False,
    )
```

```python
import numpy as np

import jax
import jax.numpy as jnp
from jax import lax
from jax.experimental import pallas as pl
from jax.experimental.pallas import tpu as pltpu
from jax.sharding import PartitionSpec as P

CELL = 128
BINS = 16
EPSILON = 1e-06
ROWS = 512
HALF = 256
QUART = 128
CHUNK = 32


def split_bf16(x):
    high = x.astype(jnp.bfloat16)
    low = (x - high.astype(jnp.float32)).astype(jnp.bfloat16)
    return high, low


def host_split(x):
    high = x.astype(np.float32).astype(jnp.bfloat16)
    low = (x - high.astype(np.float64)).astype(np.float32).astype(jnp.bfloat16)
    return high, low


def host_tables():
    k = np.arange(HALF)
    u = np.arange(QUART) + 0.5
    angle = 2 * np.pi * u[:, None] * k[None, :] / HALF
    wave = np.concatenate([np.cos(angle), np.sin(angle)], axis=0)
    high, low = host_split(wave)
    first = np.concatenate([high, high, low], axis=1)
    second = np.concatenate([high.T, high.T, low.T], axis=0)
    eight = 2 * np.pi * (np.arange(8)[:, None] * np.arange(8)[None, :] % 8) / 8
    block = np.block([[np.cos(eight), -np.sin(eight)], [np.sin(eight), np.cos(eight)]])
    high, low = host_split(block)
    octet = np.concatenate([high, high, low], axis=1)
    angle = 2 * np.pi * k[None, :] * np.array([1, 2])[:, None] / 1024
    rows = np.stack([np.cos(angle), np.sin(angle)], axis=1)
    rows = np.broadcast_to(rows[..., None], rows.shape + (128,)).astype(np.float32)
    unit = 2 * np.pi / (1 << 19)
    angle = unit * (4 * np.arange(QUART)[:, None] * np.arange(ROWS))
    between = np.stack([np.cos(angle), np.sin(angle)]).astype(np.float32)
    angle = unit * (np.array([0, 1, 2, 3, 1020, 1021, 1022, 1023])[:, None] * np.arange(ROWS))
    shift = np.stack([np.cos(angle), np.sin(angle)]).astype(np.float32)
    angle = unit * (128 * np.arange(8)[:, None] * np.arange(ROWS)[None, :])
    coarse = np.stack([np.cos(angle), np.sin(angle)]).astype(np.float32)
    angle = -2 * np.pi * k / ROWS
    lanes = np.stack([np.cos(angle), np.sin(angle)]).astype(np.float32)
    lanes = np.broadcast_to(lanes[:, None, :], (2, 8, HALF)).copy()
    return first, second, octet, rows.copy(), between, shift, coarse, lanes


def lane_butterfly(real, imag, lanes_real, lanes_imag):
    low_r, high_r = real[:, :HALF], real[:, HALF:]
    low_i, high_i = imag[:, :HALF], imag[:, HALF:]
    sum_r, sum_i = low_r + high_r, low_i + high_i
    even_r = sum_r * lanes_real - sum_i * lanes_imag
    even_i = sum_r * lanes_imag + sum_i * lanes_real
    return even_r, even_i, low_r - high_r, low_i - high_i


def split_dot(high, low, second_ref):
    return jnp.dot(
        jnp.concatenate([high, low, high], axis=1), second_ref[...], preferred_element_type=jnp.float32
    )


def encode_kernel(core_ref, strain_ref, own_real_ref, own_imag_ref, other_real_ref, other_imag_ref, rows_ref):
    rows = rows_ref.shape[1]
    for which, out_refs in enumerate(((own_real_ref, own_imag_ref), (other_real_ref, other_imag_ref))):
        segment = core_ref[0] if which == 0 else 1 - core_ref[0]
        for part in range(2):
            for row in range(rows):
                rows_ref[part, row : row + 1, :] = strain_ref[segment, part : part + 1, row * ROWS : (row + 1) * ROWS]
        data = [rows_ref[0], rows_ref[1]]
        largest = jnp.max(jnp.maximum(jnp.abs(data[0]), jnp.abs(data[1])), axis=1, keepdims=True)
        exponent = jnp.floor(jnp.log2(jnp.maximum(largest, 1e-30)) + 1.001)
        scale = jnp.exp2(15.0 - exponent)
        for value, out_ref in zip(data, out_refs):
            number = jnp.clip(jnp.round(value * scale), -32767.0, 32767.0).astype(jnp.int32)
            packed = (number[:, :HALF] << 16) | (number[:, HALF:] & 0xFFFF)
            out_ref[0, 0:rows, :] = packed[:, :128]
            out_ref[0, rows : 2 * rows, :] = packed[:, 128:]
        spread = jnp.broadcast_to(exponent.astype(jnp.int32), (rows, 128))
        same = lax.broadcasted_iota(jnp.int32, (rows, 128), 0) == lax.broadcasted_iota(jnp.int32, (rows, 128), 1)
        line = jnp.sum(jnp.where(same, spread, 0), axis=0, keepdims=True)
        out_refs[0][0, 2 * rows :, :] = jnp.broadcast_to(line, (8, 128))


def encode(core, strain):
    rows = strain.shape[2] // ROWS
    real = jax.ShapeDtypeStruct((1, 2 * rows + 8, 128), jnp.int32)
    imag = jax.ShapeDtypeStruct((1, 2 * rows, 128), jnp.int32)
    return pl.pallas_call(
        encode_kernel,
        out_shape=(real, imag, real, imag),
        in_specs=[pl.BlockSpec(memory_space=pltpu.SMEM), pl.BlockSpec(memory_space=pltpu.VMEM)],
        out_specs=(pl.BlockSpec(memory_space=pltpu.VMEM),) * 4,
        scratch_shapes=[pltpu.VMEM((2, rows, ROWS), jnp.float32)],
    )(core.reshape(1), strain)


def make_kernel(slots, real_masks, imag_masks):
    blocks = [len(masks) for masks in (real_masks, imag_masks)]

    def kernel(*refs):
        plan_ref, edge_ref, own_ref, mate_ref = refs[:4]
        real_refs = refs[4 : 4 + blocks[0]]
        imag_refs = refs[4 + blocks[0] : 4 + sum(blocks)]
        (first_ref, second_ref, octet_ref, rows_ref, base_ref, shift_ref, coarse_ref, lanes_ref, out_ref, strain_ref,
         wave_ref, between_ref, q_ref, p_ref, x_ref, o_ref, l_ref, z_ref, fold_ref, peak_ref, sem) = refs[4 + sum(blocks) :]
        live = plan_ref[slots]
        own_count = plan_ref[slots + 1]
        device = plan_ref[slots + 2]

        def fetch(step):
            slot = plan_ref[step]
            buffer = step % 2

            @pl.when(step < own_count)
            def _():
                pltpu.make_async_copy(own_ref.at[slot], wave_ref.at[buffer], sem.at[buffer]).start()

            @pl.when(step >= own_count)
            def _():
                pltpu.make_async_copy(mate_ref.at[slot - slots // 2], wave_ref.at[buffer], sem.at[buffer]).start()

        fetch(0)
        out_ref[...] = jnp.zeros_like(out_ref)

        held = imag_refs[0].shape[1] // 2
        same = lax.broadcasted_iota(jnp.int32, (held, 128), 0) == lax.broadcasted_iota(jnp.int32, (held, 128), 1)
        for part, (part_refs, masks) in enumerate(((real_refs, real_masks), (imag_refs, imag_masks))):
            for ref, group in zip(part_refs, masks):
                for i, mask in enumerate(group):
                    row = pl.multiple_of((device ^ mask) * held, held)
                    if part == 0:
                        line = jnp.broadcast_to(ref[i, 2 * held : 2 * held + 1, :], (held, 128))
                        exponent = jnp.sum(jnp.where(same, line, 0).astype(jnp.float32), axis=1, keepdims=True)
                        scale = jnp.broadcast_to(jnp.exp2(exponent - 15.0), (held, 128))
                        strain_ref[2, pl.ds(row, held), 0:128] = scale
                    scale = strain_ref[2, pl.ds(row, held), 0:128]
                    for tile in range(2):
                        word = ref[i, tile * held : (tile + 1) * held, :]
                        high = (word >> 16).astype(jnp.float32) * scale
                        low = ((word << 16) >> 16).astype(jnp.float32) * scale
                        strain_ref[part, pl.ds(row, held), tile * 128 : tile * 128 + 128] = high
                        strain_ref[part, pl.ds(row, held), HALF + tile * 128 : HALF + tile * 128 + 128] = low

        for v in range(4):
            for mirror in range(2):
                at = mirror * 4 + v
                base_r = base_ref[0]
                base_i = base_ref[1] if mirror == 0 else -base_ref[1]
                shift_r = shift_ref[0, at : at + 1, :]
                shift_i = shift_ref[1, at : at + 1, :]
                between_ref[v, mirror, 0] = base_r * shift_r - base_i * shift_i
                between_ref[v, mirror, 1] = base_r * shift_i + base_i * shift_r

        def one_slot(step, carry):
            slot = plan_ref[step]
            buffer = step % 2
            base = slot * (BINS + 1)
            first_edge = edge_ref[base]
            last_edge = edge_ref[base + BINS]

            @pl.when(step + 1 < live)
            def _():
                fetch(step + 1)

            pltpu.make_async_copy(own_ref.at[0], wave_ref.at[buffer], sem.at[buffer]).wait()

            def product(r):
                data_r = strain_ref[0, pl.ds(r, 16), :]
                data_i = strain_ref[1, pl.ds(r, 16), :]
                wave_r = wave_ref[buffer, 0, pl.ds(r, 16), :].astype(jnp.float32)
                wave_i = wave_ref[buffer, 1, pl.ds(r, 16), :].astype(jnp.float32)
                index = (
                    lax.broadcasted_iota(jnp.int32, (16, ROWS), 0) * ROWS
                    + lax.broadcasted_iota(jnp.int32, (16, ROWS), 1)
                    + r * ROWS
                )
                inside = (index >= first_edge) & (index < last_edge)
                real = jnp.where(inside, data_r * wave_r + data_i * wave_i, 0.0)
                imag = jnp.where(inside, data_i * wave_r - data_r * wave_i, 0.0)
                q_ref[0, pl.ds(r, 16), :] = real
                q_ref[1, pl.ds(r, 16), :] = imag
                p_ref[pl.ds(r, 16), :] = wave_r * wave_r + wave_i * wave_i
                return real, imag

            def front(c, carry):
                r = pl.multiple_of(c * 16, 16)
                low_r, low_i = product(r)
                high_r, high_i = product(pl.multiple_of(r + HALF, 16))
                mixed = [
                    (low_r + high_r, low_i + high_i),
                    (low_r - high_i, low_i + high_r),
                    (low_r - high_r, low_i - high_i),
                    (low_r + high_i, low_i - high_r),
                ]
                for v in range(4):
                    real, imag = mixed[v]
                    if v != 2:
                        at = (1, 0, 0, 0)[v]
                        cosine = jnp.concatenate([rows_ref[at, 0, pl.ds(r, 16), :]] * 4, axis=1)
                        sine = jnp.concatenate([rows_ref[at, 1, pl.ds(r, 16), :]] * 4, axis=1)
                        if v == 3:
                            real, imag = real * cosine - imag * sine, real * sine + imag * cosine
                        else:
                            real, imag = real * cosine + imag * sine, imag * cosine - real * sine
                    for part, value in ((0, real), (1, imag)):
                        high, low = split_bf16(value)
                        column = (2 * v + part) * ROWS
                        x_ref[pl.ds(r, 16), column : column + ROWS] = high
                        x_ref[pl.ds(pl.multiple_of(r + HALF, 16), 16), column : column + ROWS] = low
                return carry

            lax.fori_loop(0, HALF // 16, front, 0)

            offset = lax.broadcasted_iota(jnp.int32, (8, ROWS), 0) * ROWS + lax.broadcasted_iota(
                jnp.int32, (8, ROWS), 1
            )
            powers = []
            for b in range(BINS):
                lower = edge_ref[base + b]
                upper = edge_ref[base + b + 1]

                def gather(i, carry, lower=lower, upper=upper):
                    real, imag, power = carry
                    r = pl.multiple_of(i * 8, 8)
                    start = i * (8 * ROWS)
                    mask = (offset >= lower - start) & (offset < upper - start)
                    real = real + jnp.where(mask, q_ref[0, pl.ds(r, 8), :], 0.0)
                    imag = imag + jnp.where(mask, q_ref[1, pl.ds(r, 8), :], 0.0)
                    power = power + jnp.where(mask, p_ref[pl.ds(r, 8), :], 0.0)
                    return real, imag, power

                zero = jnp.zeros((8, ROWS), jnp.float32)
                real, imag, power = lax.fori_loop(
                    lower // (8 * ROWS), (upper + (8 * ROWS - 1)) // (8 * ROWS), gather, (zero, zero, zero)
                )
                fold_ref[0:8, b * ROWS : (b + 1) * ROWS] = real
                fold_ref[8:16, b * ROWS : (b + 1) * ROWS] = imag
                powers.append(jnp.sum(power, axis=(0, 1), keepdims=True))
            energy = powers[0]
            for b in range(1, BINS):
                energy = energy + powers[b]

            lanes_r = lanes_ref[0, 0:1, :]
            lanes_i = lanes_ref[1, 0:1, :]

            for v in range(4):
                column = v * 2 * ROWS
                whole = jnp.dot(
                    first_ref[...],
                    jnp.concatenate(
                        [x_ref[:, column : column + 2 * ROWS], x_ref[0:HALF, column : column + 2 * ROWS]], axis=0
                    ),
                    preferred_element_type=jnp.float32,
                )
                o_ref[...] = whole
                for chunk in range(QUART // CHUNK):
                    u = chunk * CHUNK
                    cos_r = o_ref[u : u + CHUNK, :ROWS]
                    cos_i = o_ref[u : u + CHUNK, ROWS:]
                    sin_r = o_ref[QUART + u : QUART + u + CHUNK, :ROWS]
                    sin_i = o_ref[QUART + u : QUART + u + CHUNK, ROWS:]
                    for mirror in range(2):
                        if mirror == 0:
                            real, imag = cos_r - sin_i, cos_i + sin_r
                        else:
                            real, imag = cos_r + sin_i, cos_i - sin_r
                        cosine = between_ref[v, mirror, 0, u : u + CHUNK, :]
                        sine = between_ref[v, mirror, 1, u : u + CHUNK, :]
                        real, imag = real * cosine - imag * sine, real * sine + imag * cosine
                        values = lane_butterfly(real, imag, lanes_r, lanes_i)
                        for part in range(4):
                            high, low = split_bf16(values[part])
                            at = ((chunk * 2 + mirror) * 4 + part) * CHUNK
                            l_ref[at : at + CHUNK, :HALF] = high
                            l_ref[at : at + CHUNK, HALF:] = low
                z_ref[...] = jnp.dot(
                    jnp.concatenate([l_ref[...], l_ref[:, :HALF]], axis=1),
                    second_ref[...],
                    preferred_element_type=jnp.float32,
                )
                for chunk in range(QUART // CHUNK):
                    for mirror in range(2):
                        cell = chunk if mirror == 0 else 7 - chunk
                        for parity in range(2):
                            at = ((chunk * 2 + mirror) * 4 + parity * 2) * CHUNK
                            real = z_ref[at : at + CHUNK, :]
                            imag = z_ref[at + CHUNK : at + 2 * CHUNK, :]
                            a, d = real[:, :128], real[:, 128:]
                            c, e = imag[:, :128], imag[:, 128:]
                            for side in range(2):
                                if side == 0:
                                    re, im = a - e, c + d
                                else:
                                    re, im = a + e, c - d
                                square = re * re + im * im
                                best = jnp.max(square.reshape(CHUNK // 8, 8, 128), axis=0)
                                lane = (parity * 2 + side) * 128
                                if v:
                                    best = jnp.maximum(best, peak_ref[cell, :, lane : lane + 128])
                                peak_ref[cell, :, lane : lane + 128] = best

            high, low = split_bf16(fold_ref[...])
            bands = jnp.dot(
                octet_ref[...], jnp.concatenate([high, low, high], axis=0), preferred_element_type=jnp.float32
            )
            parts = [[], [], [], []]
            coarse_r = coarse_ref[0]
            coarse_i = coarse_ref[1]
            for b in range(BINS):
                real = bands[0:8, b * ROWS : (b + 1) * ROWS]
                imag = bands[8:16, b * ROWS : (b + 1) * ROWS]
                real, imag = real * coarse_r - imag * coarse_i, real * coarse_i + imag * coarse_r
                values = lane_butterfly(real, imag, lanes_r, lanes_i)
                for part in range(4):
                    parts[part].append(values[part])
            left = jnp.concatenate([value for part in parts for value in part], axis=0)
            high, low = split_bf16(left)
            result = split_dot(high, low, second_ref)
            loud = jnp.concatenate(
                [jnp.max(peak_ref[cell], axis=0, keepdims=True) for cell in range(8)], axis=0
            )
            inverse = 1.0 / energy
            top = jnp.zeros((8, 128), jnp.float32)
            for parity in range(2):
                real = result[parity * 256 : parity * 256 + 128, :]
                imag = result[parity * 256 + 128 : parity * 256 + 256, :]
                a, d = real[:, :128], real[:, 128:]
                c, e = imag[:, :128], imag[:, 128:]
                for side in range(2):
                    if side == 0:
                        re, im = a - e, c + d
                    else:
                        re, im = a + e, c - d
                    re = re.reshape(BINS, 8, 128)
                    im = im.reshape(BINS, 8, 128)
                    total_r = jnp.sum(re, axis=0)
                    total_i = jnp.sum(im, axis=0)
                    misfit = jnp.zeros((8, 128), jnp.float32)
                    for b in range(BINS):
                        weight = powers[b] * inverse
                        error_r = re[b] - weight * total_r
                        error_i = im[b] - weight * total_i
                        misfit = misfit + (error_r * error_r + error_i * error_i) * (1.0 / (powers[b] + EPSILON))
                    reduced = misfit / (2 * BINS - 2)
                    factor = jnp.where(
                        reduced > 1.0, jnp.exp(jnp.log((1.0 + reduced * reduced * reduced) / 2.0) * (-1.0 / 6.0)), 1.0
                    )
                    lane = (parity * 2 + side) * 128
                    top = jnp.maximum(top, jnp.sqrt(loud[:, lane : lane + 128]) * factor)
            best = jnp.max(top, axis=(0, 1), keepdims=True) / jnp.sqrt(energy)
            out_ref[pl.ds(slot, 1), :] = jnp.broadcast_to(best, (1, 128))
            return carry

        lax.fori_loop(0, live, one_slot, 0)

    return kernel


def slot_peaks(plan, edges, own_waves, mate_waves, real_blocks, imag_blocks, real_masks, imag_masks):
    slots = 2 * own_waves.shape[0]
    tables = [jnp.asarray(table) for table in host_tables()]
    smem = pl.BlockSpec(memory_space=pltpu.SMEM)
    hbm = pl.BlockSpec(memory_space=pl.ANY)
    vmem = pl.BlockSpec(memory_space=pltpu.VMEM)
    return pl.pallas_call(
        make_kernel(slots, real_masks, imag_masks),
        out_shape=jax.ShapeDtypeStruct((slots, 128), jnp.float32),
        in_specs=[smem, smem, hbm, hbm] + [vmem] * (len(real_blocks) + len(imag_blocks) + len(tables)),
        out_specs=vmem,
        scratch_shapes=[
            pltpu.VMEM((3, ROWS, ROWS), jnp.float32),
            pltpu.VMEM((2, 2, ROWS, ROWS), jnp.bfloat16),
            pltpu.VMEM((4, 2, 2, QUART, ROWS), jnp.float32),
            pltpu.VMEM((2, ROWS, ROWS), jnp.float32),
            pltpu.VMEM((ROWS, ROWS), jnp.float32),
            pltpu.VMEM((ROWS, 8 * ROWS), jnp.bfloat16),
            pltpu.VMEM((HALF, 2 * ROWS), jnp.float32),
            pltpu.VMEM((1024, ROWS), jnp.bfloat16),
            pltpu.VMEM((1024, HALF), jnp.float32),
            pltpu.VMEM((16, BINS * ROWS), jnp.float32),
            pltpu.VMEM((8, 8, ROWS), jnp.float32),
            pltpu.SemaphoreType.DMA((2,)),
        ],
        compiler_params=pltpu.CompilerParams(vmem_limit_bytes=48 << 20),
    )(plan, edges, own_waves, mate_waves, *real_blocks, *imag_blocks, *tables)


def exchange(x, bit):
    devices = lax.axis_size("bank")
    return lax.ppermute(x, "bank", [(i, i ^ bit) for i in range(devices)])


def per_device(strain, templates, counts, edges):
    devices = lax.axis_size("bank")
    device = lax.axis_index("bank").astype(jnp.int32)
    core = device % 2
    slots = templates.shape[0]
    bits = [1 << i for i in range(1, devices.bit_length() - 1)]
    orders = [bits[::-1], bits[:1] + bits[:0:-1]]

    own_real, own_imag, other_real, other_imag = encode(core, strain)
    current = [
        jnp.concatenate([own, exchange(other, 1)]) for own, other in ((own_real, other_real), (own_imag, other_imag))
    ]
    templates, *current = lax.optimization_barrier((templates, *current))
    mate_waves = exchange(templates, 1).reshape(slots, 2, ROWS, ROWS)
    own_waves = templates.reshape(slots, 2, ROWS, ROWS)
    masks = [[0, 1], [0, 1]]
    for level in range(len(bits)):
        arrived = [exchange(current[half], orders[half][level]) for half in range(2)]
        added = [[m ^ orders[half][level] for m in masks[half]] for half in range(2)]
        if level + 1 < len(bits):
            current = [jnp.concatenate([current[half], arrived[half]]) for half in range(2)]
            masks = [masks[half] + added[half] for half in range(2)]
        if level + 2 == len(bits):
            own_waves, *current = lax.optimization_barrier((own_waves, *current))
    blocks = [[current[half], arrived[half]] for half in range(2)]
    block_masks = [[masks[half], added[half]] for half in range(2)]

    small = jnp.concatenate([counts, edges.reshape(-1)])
    mate_small = exchange(small, 1)
    own_count = small[0]
    live = own_count + mate_small[0]
    ramp = jnp.minimum(jnp.arange(2 * slots, dtype=jnp.int32), live - 1)
    order = jnp.where(ramp < own_count, ramp, slots + ramp - own_count)
    plan = jnp.concatenate([order, live[None], own_count[None], device[None]]).astype(jnp.int32)
    all_edges = jnp.concatenate([small[1:], mate_small[1:]])
    peaks = slot_peaks(plan, all_edges, own_waves, mate_waves, *blocks, *block_masks)

    mine = lax.broadcasted_iota(jnp.int32, peaks.shape, 1) % 2 == core
    arrived = exchange(peaks, 1)
    swapped = jnp.concatenate([arrived[slots:], arrived[:slots]])
    both = jnp.where(mine, peaks, swapped)
    best = both
    for bit in bits:
        best = jnp.maximum(best, exchange(best, bit))
    return (both[:slots, :2], jnp.max(best, axis=0)[:2])


def solution(mesh):
    placed = (P("seg", None, "bank"), P("bank", None, None), P("bank"), P("bank", None))
    return jax.shard_map(
        per_device,
        mesh=mesh,
        in_specs=placed,
        out_specs=(P("bank", "seg"), P("seg")),
        check_vma=False,
    )
```

```python
import numpy as np

import jax
import jax.numpy as jnp
from jax import lax
from jax.experimental import pallas as pl
from jax.experimental.pallas import tpu as pltpu
from jax.sharding import PartitionSpec as P

CELL = 128
BINS = 16
EPSILON = 1e-06
ROWS = 512
HALF = 256
QUART = 128
CHUNK = 32


def split_bf16(x):
    high = x.astype(jnp.bfloat16)
    low = (x - high.astype(jnp.float32)).astype(jnp.bfloat16)
    return high, low


def host_split(x):
    high = x.astype(np.float32).astype(jnp.bfloat16)
    low = (x - high.astype(np.float64)).astype(np.float32).astype(jnp.bfloat16)
    return high, low


def host_tables():
    k = np.arange(HALF)
    u = np.arange(QUART) + 0.5
    angle = 2 * np.pi * u[:, None] * k[None, :] / HALF
    wave = np.concatenate([np.cos(angle), np.sin(angle)], axis=0)
    high, low = host_split(wave)
    first = np.concatenate([high, high, low], axis=1)
    second = np.concatenate([high.T, high.T, low.T], axis=0)
    eight = 2 * np.pi * (np.arange(8)[:, None] * np.arange(8)[None, :] % 8) / 8
    block = np.block([[np.cos(eight), -np.sin(eight)], [np.sin(eight), np.cos(eight)]])
    high, low = host_split(block)
    octet = np.concatenate([high, high, low], axis=1)
    angle = 2 * np.pi * k[None, :] * np.array([1, 2])[:, None] / 1024
    rows = np.stack([np.cos(angle), np.sin(angle)], axis=1)
    rows = np.broadcast_to(rows[..., None], rows.shape + (128,)).astype(np.float32)
    unit = 2 * np.pi / (1 << 19)
    angle = unit * (4 * np.arange(QUART)[:, None] * np.arange(ROWS))
    between = np.stack([np.cos(angle), np.sin(angle)]).astype(np.float32)
    angle = unit * (np.array([0, 1, 2, 3, 1020, 1021, 1022, 1023])[:, None] * np.arange(ROWS))
    shift = np.stack([np.cos(angle), np.sin(angle)]).astype(np.float32)
    angle = unit * (128 * np.arange(8)[:, None] * np.arange(ROWS)[None, :])
    coarse = np.stack([np.cos(angle), np.sin(angle)]).astype(np.float32)
    angle = -2 * np.pi * k / ROWS
    lanes = np.stack([np.cos(angle), np.sin(angle)]).astype(np.float32)
    lanes = np.broadcast_to(lanes[:, None, :], (2, 8, HALF)).copy()
    return first, second, octet, rows.copy(), between, shift, coarse, lanes


def lane_butterfly(real, imag, lanes_real, lanes_imag):
    low_r, high_r = real[:, :HALF], real[:, HALF:]
    low_i, high_i = imag[:, :HALF], imag[:, HALF:]
    sum_r, sum_i = low_r + high_r, low_i + high_i
    even_r = sum_r * lanes_real - sum_i * lanes_imag
    even_i = sum_r * lanes_imag + sum_i * lanes_real
    return even_r, even_i, low_r - high_r, low_i - high_i


def encode_kernel(core_ref, strain_ref, own_real_ref, own_imag_ref, other_real_ref, other_imag_ref, rows_ref):
    rows = rows_ref.shape[1]
    for which, out_refs in enumerate(((own_real_ref, own_imag_ref), (other_real_ref, other_imag_ref))):
        segment = core_ref[0] if which == 0 else 1 - core_ref[0]
        for part in range(2):
            for row in range(rows):
                rows_ref[part, row : row + 1, :] = strain_ref[segment, part : part + 1, row * ROWS : (row + 1) * ROWS]
        data = [rows_ref[0], rows_ref[1]]
        largest = jnp.max(jnp.maximum(jnp.abs(data[0]), jnp.abs(data[1])), axis=1, keepdims=True)
        exponent = jnp.floor(jnp.log2(jnp.maximum(largest, 1e-30)) + 1.001)
        scale = jnp.exp2(15.0 - exponent)
        for value, out_ref in zip(data, out_refs):
            number = jnp.clip(jnp.round(value * scale), -32767.0, 32767.0).astype(jnp.int32)
            packed = (number[:, :HALF] << 16) | (number[:, HALF:] & 0xFFFF)
            out_ref[0, 0:rows, :] = packed[:, :128]
            out_ref[0, rows : 2 * rows, :] = packed[:, 128:]
        spread = jnp.broadcast_to(exponent.astype(jnp.int32), (rows, 128))
        same = lax.broadcasted_iota(jnp.int32, (rows, 128), 0) == lax.broadcasted_iota(jnp.int32, (rows, 128), 1)
        line = jnp.sum(jnp.where(same, spread, 0), axis=0, keepdims=True)
        out_refs[0][0, 2 * rows :, :] = jnp.broadcast_to(line, (8, 128))


def encode(core, strain):
    rows = strain.shape[2] // ROWS
    real = jax.ShapeDtypeStruct((1, 2 * rows + 8, 128), jnp.int32)
    imag = jax.ShapeDtypeStruct((1, 2 * rows, 128), jnp.int32)
    return pl.pallas_call(
        encode_kernel,
        out_shape=(real, imag, real, imag),
        in_specs=[pl.BlockSpec(memory_space=pltpu.SMEM), pl.BlockSpec(memory_space=pltpu.VMEM)],
        out_specs=(pl.BlockSpec(memory_space=pltpu.VMEM),) * 4,
        scratch_shapes=[pltpu.VMEM((2, rows, ROWS), jnp.float32)],
    )(core.reshape(1), strain)


def make_kernel(slots, real_masks, imag_masks):
    blocks = [len(masks) for masks in (real_masks, imag_masks)]

    def kernel(*refs):
        plan_ref, edge_ref, own_ref, mate_ref = refs[:4]
        real_refs = refs[4 : 4 + blocks[0]]
        imag_refs = refs[4 + blocks[0] : 4 + sum(blocks)]
        (first_ref, second_ref, octet_ref, rows_ref, base_ref, shift_ref, coarse_ref, lanes_ref, out_ref, strain_ref,
         wave_ref, between_ref, q_ref, p_ref, x_ref, o_ref, l_ref, z_ref, fold_ref, peak_ref, power_ref, sem) = refs[4 + sum(blocks) :]
        live = plan_ref[slots]
        own_count = plan_ref[slots + 1]
        device = plan_ref[slots + 2]

        def fetch(step):
            slot = plan_ref[step]
            buffer = step % 2

            @pl.when(step < own_count)
            def _():
                pltpu.make_async_copy(own_ref.at[slot], wave_ref.at[buffer], sem.at[buffer]).start()

            @pl.when(step >= own_count)
            def _():
                pltpu.make_async_copy(mate_ref.at[slot - slots // 2], wave_ref.at[buffer], sem.at[buffer]).start()

        fetch(0)
        out_ref[...] = jnp.zeros_like(out_ref)

        held = imag_refs[0].shape[1] // 2
        same = lax.broadcasted_iota(jnp.int32, (held, 128), 0) == lax.broadcasted_iota(jnp.int32, (held, 128), 1)
        for part, (part_refs, masks) in enumerate(((real_refs, real_masks), (imag_refs, imag_masks))):
            for ref, group in zip(part_refs, masks):
                for i, mask in enumerate(group):
                    row = pl.multiple_of((device ^ mask) * held, held)
                    if part == 0:
                        line = jnp.broadcast_to(ref[i, 2 * held : 2 * held + 1, :], (held, 128))
                        exponent = jnp.sum(jnp.where(same, line, 0).astype(jnp.float32), axis=1, keepdims=True)
                        scale = jnp.broadcast_to(jnp.exp2(exponent - 15.0), (held, 128))
                        strain_ref[2, pl.ds(row, held), 0:128] = scale
                    scale = strain_ref[2, pl.ds(row, held), 0:128]
                    for tile in range(2):
                        word = ref[i, tile * held : (tile + 1) * held, :]
                        high = (word >> 16).astype(jnp.float32) * scale
                        low = ((word << 16) >> 16).astype(jnp.float32) * scale
                        strain_ref[part, pl.ds(row, held), tile * 128 : tile * 128 + 128] = high
                        strain_ref[part, pl.ds(row, held), HALF + tile * 128 : HALF + tile * 128 + 128] = low

        for v in range(4):
            for mirror in range(2):
                at = mirror * 4 + v
                base_r = base_ref[0]
                base_i = base_ref[1] if mirror == 0 else -base_ref[1]
                shift_r = shift_ref[0, at : at + 1, :]
                shift_i = shift_ref[1, at : at + 1, :]
                between_ref[v, mirror, 0] = base_r * shift_r - base_i * shift_i
                between_ref[v, mirror, 1] = base_r * shift_i + base_i * shift_r

        def one_slot(step, carry):
            slot = plan_ref[step]
            buffer = step % 2
            base = slot * (BINS + 1)
            first_edge = edge_ref[base]
            last_edge = edge_ref[base + BINS]

            @pl.when(step + 1 < live)
            def _():
                fetch(step + 1)

            pltpu.make_async_copy(own_ref.at[0], wave_ref.at[buffer], sem.at[buffer]).wait()

            def trim(r):
                start = r * ROWS

                @pl.when((start < first_edge) | (start + 16 * ROWS > last_edge))
                def _():
                    index = lax.broadcasted_iota(jnp.int32, (16, ROWS), 0) * ROWS + lax.broadcasted_iota(
                        jnp.int32, (16, ROWS), 1
                    )
                    inside = (index >= first_edge - start) & (index < last_edge - start)
                    for part in range(2):
                        wave = wave_ref[buffer, part, pl.ds(r, 16), :].astype(jnp.float32)
                        wave_ref[buffer, part, pl.ds(r, 16), :] = jnp.where(inside, wave, 0.0).astype(jnp.bfloat16)

            def product(r, lane):
                data_r = strain_ref[0, pl.ds(r, 16), lane : lane + 128]
                data_i = strain_ref[1, pl.ds(r, 16), lane : lane + 128]
                wave_r = wave_ref[buffer, 0, pl.ds(r, 16), lane : lane + 128].astype(jnp.float32)
                wave_i = wave_ref[buffer, 1, pl.ds(r, 16), lane : lane + 128].astype(jnp.float32)
                real = data_r * wave_r + data_i * wave_i
                imag = data_i * wave_r - data_r * wave_i
                q_ref[0, pl.ds(r, 16), lane : lane + 128] = real
                q_ref[1, pl.ds(r, 16), lane : lane + 128] = imag
                p_ref[pl.ds(r, 16), lane : lane + 128] = wave_r * wave_r + wave_i * wave_i
                return real, imag

            def front(c, carry):
                r = pl.multiple_of(c * 16, 16)
                above = pl.multiple_of(r + HALF, 16)
                for lane in range(0, ROWS, 128):
                    low_r, low_i = product(r, lane)
                    high_r, high_i = product(above, lane)
                    mixed = [
                        (low_r + high_r, low_i + high_i),
                        (low_r - high_i, low_i + high_r),
                        (low_r - high_r, low_i - high_i),
                        (low_r + high_i, low_i - high_r),
                    ]
                    for v in range(4):
                        real, imag = mixed[v]
                        if v != 2:
                            at = (1, 0, 0, 0)[v]
                            cosine = rows_ref[at, 0, pl.ds(r, 16), :]
                            sine = rows_ref[at, 1, pl.ds(r, 16), :]
                            if v == 3:
                                real, imag = real * cosine - imag * sine, real * sine + imag * cosine
                            else:
                                real, imag = real * cosine + imag * sine, imag * cosine - real * sine
                        for part, value in ((0, real), (1, imag)):
                            high, low = split_bf16(value)
                            column = (2 * v + part) * ROWS + lane
                            x_ref[pl.ds(r, 16), column : column + 128] = high
                            x_ref[pl.ds(above, 16), column : column + 128] = low
                return carry

            def clear(c, carry):
                trim(pl.multiple_of(c * 16, 16))
                return carry

            lax.fori_loop(0, first_edge // (16 * ROWS) + 1, clear, 0)
            lax.fori_loop(last_edge // (16 * ROWS), ROWS // 16, clear, 0)
            lax.fori_loop(0, HALF // 16, front, 0, unroll=2)

            offset = lax.broadcasted_iota(jnp.int32, (8, ROWS), 0) * ROWS + lax.broadcasted_iota(
                jnp.int32, (8, ROWS), 1
            )
            for b in range(BINS):
                lower = edge_ref[base + b]
                upper = edge_ref[base + b + 1]

                def gather(i, carry, lower=lower, upper=upper):
                    real, imag, power = carry
                    r = pl.multiple_of(i * 8, 8)
                    start = i * (8 * ROWS)
                    mask = (offset >= lower - start) & (offset < upper - start)
                    real = real + jnp.where(mask, q_ref[0, pl.ds(r, 8), :], 0.0)
                    imag = imag + jnp.where(mask, q_ref[1, pl.ds(r, 8), :], 0.0)
                    power = power + jnp.where(mask, p_ref[pl.ds(r, 8), :], 0.0)
                    return real, imag, power

                zero = jnp.zeros((8, ROWS), jnp.float32)
                real, imag, power = lax.fori_loop(
                    lower // (8 * ROWS), (upper + (8 * ROWS - 1)) // (8 * ROWS), gather, (zero, zero, zero)
                )
                fold_ref[0:8, b * ROWS : (b + 1) * ROWS] = real
                fold_ref[8:16, b * ROWS : (b + 1) * ROWS] = imag
                power_ref[8 * b : 8 * b + 8, :] = (
                    power[:, :128] + power[:, 128:256] + power[:, 256:384] + power[:, 384:]
                )
            power = jnp.sum(jnp.sum(power_ref[...].reshape(BINS, 8, 128), axis=1), axis=1, keepdims=True)
            energy = jnp.sum(power, axis=0, keepdims=True)
            weight = jnp.broadcast_to(power / energy, (BINS, 128))
            inverse = jnp.broadcast_to(1.0 / (power + EPSILON), (BINS, 128))


            def rows_stage(v, j):
                column = v * 2 * ROWS + j * HALF
                o_ref[v % 2, :, j * HALF : (j + 1) * HALF] = jnp.dot(
                    first_ref[...],
                    jnp.concatenate([x_ref[:, column : column + HALF], x_ref[0:HALF, column : column + HALF]], axis=0),
                    preferred_element_type=jnp.float32,
                )

            def middle(v, chunk):
                u = chunk * CHUNK
                cos_r = o_ref[v % 2, u : u + CHUNK, :ROWS]
                cos_i = o_ref[v % 2, u : u + CHUNK, ROWS:]
                sin_r = o_ref[v % 2, QUART + u : QUART + u + CHUNK, :ROWS]
                sin_i = o_ref[v % 2, QUART + u : QUART + u + CHUNK, ROWS:]
                for mirror in range(2):
                    if mirror == 0:
                        real, imag = cos_r - sin_i, cos_i + sin_r
                    else:
                        real, imag = cos_r + sin_i, cos_i - sin_r
                    cosine = between_ref[v, mirror, 0, u : u + CHUNK, :]
                    sine = between_ref[v, mirror, 1, u : u + CHUNK, :]
                    real, imag = real * cosine - imag * sine, real * sine + imag * cosine
                    values = lane_butterfly(real, imag, lanes_ref[0, 0:1, :], lanes_ref[1, 0:1, :])
                    for part in range(4):
                        high, low = split_bf16(values[part])
                        at = ((chunk * 2 + mirror) * 4 + part) * CHUNK
                        l_ref[v % 2, at : at + CHUNK, :HALF] = high
                        l_ref[v % 2, at : at + CHUNK, HALF:] = low

            def columns_stage(v, chunk):
                at = chunk * 8 * CHUNK
                z_ref[v % 2, at : at + 8 * CHUNK, :] = jnp.dot(
                    jnp.concatenate(
                        [l_ref[v % 2, at : at + 8 * CHUNK, :], l_ref[v % 2, at : at + 8 * CHUNK, :HALF]], axis=1
                    ),
                    second_ref[...],
                    preferred_element_type=jnp.float32,
                )

            def finish(v, chunk):
                for mirror in range(2):
                    cell = chunk if mirror == 0 else 7 - chunk
                    for parity in range(2):
                        at = ((chunk * 2 + mirror) * 4 + parity * 2) * CHUNK
                        real = z_ref[v % 2, at : at + CHUNK, :]
                        imag = z_ref[v % 2, at + CHUNK : at + 2 * CHUNK, :]
                        a, d = real[:, :128], real[:, 128:]
                        c, e = imag[:, :128], imag[:, 128:]
                        for side in range(2):
                            if side == 0:
                                re, im = a - e, c + d
                            else:
                                re, im = a + e, c - d
                            square = re * re + im * im
                            best = jnp.max(square.reshape(CHUNK // 8, 8, 128), axis=0)
                            lane = (parity * 2 + side) * 128
                            if v:
                                best = jnp.maximum(best, peak_ref[cell, :, lane : lane + 128])
                            peak_ref[cell, :, lane : lane + 128] = best

            for turn in range(6):
                for j in range(4):
                    if turn < 4:
                        rows_stage(turn, j)
                    if 2 <= turn:
                        columns_stage(turn - 2, j)
                    if 1 <= turn < 5:
                        middle(turn - 1, j)
                    if 2 <= turn:
                        finish(turn - 2, j)

            coarse_r = jnp.concatenate([coarse_ref[0], coarse_ref[0]], axis=0)
            coarse_i = jnp.concatenate([coarse_ref[1], coarse_ref[1]], axis=0)
            for b in range(0, BINS, 2):
                high, low = split_bf16(fold_ref[:, b * ROWS : (b + 2) * ROWS])
                bands = jnp.dot(
                    octet_ref[...], jnp.concatenate([high, low, high], axis=0), preferred_element_type=jnp.float32
                )
                real = jnp.concatenate([bands[0:8, :ROWS], bands[0:8, ROWS:]], axis=0)
                imag = jnp.concatenate([bands[8:16, :ROWS], bands[8:16, ROWS:]], axis=0)
                real, imag = real * coarse_r - imag * coarse_i, real * coarse_i + imag * coarse_r
                values = lane_butterfly(real, imag, lanes_ref[0, 0:1, :], lanes_ref[1, 0:1, :])
                for part in range(4):
                    high, low = split_bf16(values[part])
                    at = part * 128 + b * 8
                    l_ref[0, at : at + 16, :HALF] = high
                    l_ref[0, at : at + 16, HALF:] = low
            z_ref[0, 0:512, :] = jnp.dot(
                jnp.concatenate([l_ref[0, 0:512, :], l_ref[0, 0:512, :HALF]], axis=1),
                second_ref[...],
                preferred_element_type=jnp.float32,
            )
            loud = jnp.concatenate(
                [jnp.max(peak_ref[cell], axis=0, keepdims=True) for cell in range(8)], axis=0
            )
            top = jnp.zeros((8, 128), jnp.float32)
            for parity in range(2):
                real = z_ref[0, parity * 256 : parity * 256 + 128, :]
                imag = z_ref[0, parity * 256 + 128 : parity * 256 + 256, :]
                a, d = real[:, :128], real[:, 128:]
                c, e = imag[:, :128], imag[:, 128:]
                for side in range(2):
                    if side == 0:
                        re, im = a - e, c + d
                    else:
                        re, im = a + e, c - d
                    re = re.reshape(BINS, 8, 128)
                    im = im.reshape(BINS, 8, 128)
                    total_r = jnp.sum(re, axis=0)
                    total_i = jnp.sum(im, axis=0)
                    misfit = jnp.zeros((8, 128), jnp.float32)
                    for b in range(BINS):
                        error_r = re[b] - weight[b : b + 1] * total_r
                        error_i = im[b] - weight[b : b + 1] * total_i
                        misfit = misfit + (error_r * error_r + error_i * error_i) * inverse[b : b + 1]
                    reduced = misfit / (2 * BINS - 2)
                    factor = jnp.where(
                        reduced > 1.0, jnp.exp(jnp.log((1.0 + reduced * reduced * reduced) / 2.0) * (-1.0 / 6.0)), 1.0
                    )
                    lane = (parity * 2 + side) * 128
                    top = jnp.maximum(top, jnp.sqrt(loud[:, lane : lane + 128]) * factor)
            best = jnp.max(top, axis=(0, 1), keepdims=True) / jnp.sqrt(energy)
            out_ref[pl.ds(slot, 1), :] = jnp.broadcast_to(best, (1, 128))
            return carry

        lax.fori_loop(0, live, one_slot, 0)

    return kernel


def slot_peaks(plan, edges, own_waves, mate_waves, real_blocks, imag_blocks, real_masks, imag_masks):
    slots = 2 * own_waves.shape[0]
    tables = [jnp.asarray(table) for table in host_tables()]
    smem = pl.BlockSpec(memory_space=pltpu.SMEM)
    hbm = pl.BlockSpec(memory_space=pl.ANY)
    vmem = pl.BlockSpec(memory_space=pltpu.VMEM)
    return pl.pallas_call(
        make_kernel(slots, real_masks, imag_masks),
        out_shape=jax.ShapeDtypeStruct((slots, 128), jnp.float32),
        in_specs=[smem, smem, hbm, hbm] + [vmem] * (len(real_blocks) + len(imag_blocks) + len(tables)),
        out_specs=vmem,
        scratch_shapes=[
            pltpu.VMEM((3, ROWS, ROWS), jnp.float32),
            pltpu.VMEM((2, 2, ROWS, ROWS), jnp.bfloat16),
            pltpu.VMEM((4, 2, 2, QUART, ROWS), jnp.float32),
            pltpu.VMEM((2, ROWS, ROWS), jnp.float32),
            pltpu.VMEM((ROWS, ROWS), jnp.float32),
            pltpu.VMEM((ROWS, 8 * ROWS), jnp.bfloat16),
            pltpu.VMEM((2, HALF, 2 * ROWS), jnp.float32),
            pltpu.VMEM((2, 1024, ROWS), jnp.bfloat16),
            pltpu.VMEM((2, 1024, HALF), jnp.float32),
            pltpu.VMEM((16, BINS * ROWS), jnp.float32),
            pltpu.VMEM((8, 8, ROWS), jnp.float32),
            pltpu.VMEM((8 * BINS, 128), jnp.float32),
            pltpu.SemaphoreType.DMA((2,)),
        ],
        compiler_params=pltpu.CompilerParams(vmem_limit_bytes=48 << 20),
    )(plan, edges, own_waves, mate_waves, *real_blocks, *imag_blocks, *tables)


def exchange(x, bit):
    devices = lax.axis_size("bank")
    return lax.ppermute(x, "bank", [(i, i ^ bit) for i in range(devices)])


def per_device(strain, templates, counts, edges):
    devices = lax.axis_size("bank")
    device = lax.axis_index("bank").astype(jnp.int32)
    core = device % 2
    slots = templates.shape[0]
    bits = [1 << i for i in range(1, devices.bit_length() - 1)]
    orders = [bits[::-1], bits[:1] + bits[:0:-1]]

    own_real, own_imag, other_real, other_imag = encode(core, strain)
    current = [
        jnp.concatenate([own, exchange(other, 1)]) for own, other in ((own_real, other_real), (own_imag, other_imag))
    ]
    templates, *current = lax.optimization_barrier((templates, *current))
    mate_waves = exchange(templates, 1).reshape(slots, 2, ROWS, ROWS)
    own_waves = templates.reshape(slots, 2, ROWS, ROWS)
    masks = [[0, 1], [0, 1]]
    for level in range(len(bits)):
        arrived = [exchange(current[half], orders[half][level]) for half in range(2)]
        added = [[m ^ orders[half][level] for m in masks[half]] for half in range(2)]
        if level + 1 < len(bits):
            current = [jnp.concatenate([current[half], arrived[half]]) for half in range(2)]
            masks = [masks[half] + added[half] for half in range(2)]
        if level + 2 == len(bits):
            own_waves, *current = lax.optimization_barrier((own_waves, *current))
    blocks = [[current[half], arrived[half]] for half in range(2)]
    block_masks = [[masks[half], added[half]] for half in range(2)]

    small = jnp.concatenate([counts, edges.reshape(-1)])
    mate_small = exchange(small, 1)
    own_count = small[0]
    live = own_count + mate_small[0]
    ramp = jnp.minimum(jnp.arange(2 * slots, dtype=jnp.int32), live - 1)
    order = jnp.where(ramp < own_count, ramp, slots + ramp - own_count)
    plan = jnp.concatenate([order, live[None], own_count[None], device[None]]).astype(jnp.int32)
    all_edges = jnp.concatenate([small[1:], mate_small[1:]])
    peaks = slot_peaks(plan, all_edges, own_waves, mate_waves, *blocks, *block_masks)

    mine = lax.broadcasted_iota(jnp.int32, peaks.shape, 1) % 2 == core
    arrived = exchange(peaks, 1)
    swapped = jnp.concatenate([arrived[slots:], arrived[:slots]])
    both = jnp.where(mine, peaks, swapped)
    best = both
    for bit in bits:
        best = jnp.maximum(best, exchange(best, bit))
    return (both[:slots, :2], jnp.max(best, axis=0)[:2])


def solution(mesh):
    placed = (P("seg", None, "bank"), P("bank", None, None), P("bank"), P("bank", None))
    return jax.shard_map(
        per_device,
        mesh=mesh,
        in_specs=placed,
        out_specs=(P("bank", "seg"), P("seg")),
        check_vma=False,
    )
```

```python
import numpy as np

import jax
import jax.numpy as jnp
from jax import lax
from jax.experimental import pallas as pl
from jax.experimental.pallas import tpu as pltpu
from jax.sharding import PartitionSpec as P

CELL = 128
BINS = 16
EPSILON = 1e-06
ROWS = 512
HALF = 256
QUART = 128
CHUNK = 32


def split_bf16(x):
    high = x.astype(jnp.bfloat16)
    low = (x - high.astype(jnp.float32)).astype(jnp.bfloat16)
    return high, low


def host_split(x):
    high = x.astype(np.float32).astype(jnp.bfloat16)
    low = (x - high.astype(np.float64)).astype(np.float32).astype(jnp.bfloat16)
    return high, low


def host_tables():
    k = np.arange(HALF)
    u = np.arange(QUART) + 0.5
    angle = 2 * np.pi * u[:, None] * k[None, :] / HALF
    wave = np.concatenate([np.cos(angle), np.sin(angle)], axis=0)
    high, low = host_split(wave)
    first = np.concatenate([high, high, low], axis=1)
    second = np.concatenate([high.T, high.T, low.T], axis=0)
    eight = 2 * np.pi * (np.arange(8)[:, None] * np.arange(8)[None, :] % 8) / 8
    block = np.block([[np.cos(eight), -np.sin(eight)], [np.sin(eight), np.cos(eight)]])
    high, low = host_split(block)
    octet = np.concatenate([high, high, low], axis=1)
    angle = 2 * np.pi * k[None, :] * np.array([1, 2])[:, None] / 1024
    rows = np.stack([np.cos(angle), np.sin(angle)], axis=1)
    rows = np.broadcast_to(rows[..., None], rows.shape + (128,)).astype(np.float32)
    unit = 2 * np.pi / (1 << 19)
    angle = unit * (4 * np.arange(QUART)[:, None] * np.arange(ROWS))
    between = np.stack([np.cos(angle), np.sin(angle)]).astype(np.float32)
    angle = unit * (np.array([0, 1, 2, 3, 1020, 1021, 1022, 1023])[:, None] * np.arange(ROWS))
    shift = np.stack([np.cos(angle), np.sin(angle)]).astype(np.float32)
    angle = unit * (128 * np.arange(8)[:, None] * np.arange(ROWS)[None, :])
    coarse = np.stack([np.cos(angle), np.sin(angle)]).astype(np.float32)
    angle = -2 * np.pi * k / ROWS
    lanes = np.stack([np.cos(angle), np.sin(angle)]).astype(np.float32)
    lanes = np.broadcast_to(lanes[:, None, :], (2, 8, HALF)).copy()
    return first, second, octet, rows.copy(), between, shift, coarse, lanes


def lane_butterfly(real, imag, lanes_real, lanes_imag):
    low_r, high_r = real[:, :HALF], real[:, HALF:]
    low_i, high_i = imag[:, :HALF], imag[:, HALF:]
    sum_r, sum_i = low_r + high_r, low_i + high_i
    even_r = sum_r * lanes_real - sum_i * lanes_imag
    even_i = sum_r * lanes_imag + sum_i * lanes_real
    return even_r, even_i, low_r - high_r, low_i - high_i


def encode_kernel(core_ref, strain_ref, own_real_ref, own_imag_ref, other_real_ref, other_imag_ref, rows_ref):
    rows = rows_ref.shape[1]
    for which, out_refs in enumerate(((own_real_ref, own_imag_ref), (other_real_ref, other_imag_ref))):
        segment = core_ref[0] if which == 0 else 1 - core_ref[0]
        for part in range(2):
            for row in range(rows):
                rows_ref[part, row : row + 1, :] = strain_ref[segment, part : part + 1, row * ROWS : (row + 1) * ROWS]
        data = [rows_ref[0], rows_ref[1]]
        largest = jnp.max(jnp.maximum(jnp.abs(data[0]), jnp.abs(data[1])), axis=1, keepdims=True)
        exponent = jnp.floor(jnp.log2(jnp.maximum(largest, 1e-30)) + 1.001)
        scale = jnp.exp2(15.0 - exponent)
        for value, out_ref in zip(data, out_refs):
            number = jnp.clip(jnp.round(value * scale), -32767.0, 32767.0).astype(jnp.int32)
            packed = (number[:, :HALF] << 16) | (number[:, HALF:] & 0xFFFF)
            out_ref[0, 0:rows, :] = packed[:, :128]
            out_ref[0, rows : 2 * rows, :] = packed[:, 128:]
        spread = jnp.broadcast_to(exponent.astype(jnp.int32), (rows, 128))
        same = lax.broadcasted_iota(jnp.int32, (rows, 128), 0) == lax.broadcasted_iota(jnp.int32, (rows, 128), 1)
        line = jnp.sum(jnp.where(same, spread, 0), axis=0, keepdims=True)
        out_refs[0][0, 2 * rows :, :] = jnp.broadcast_to(line, (8, 128))


def encode(core, strain):
    rows = strain.shape[2] // ROWS
    real = jax.ShapeDtypeStruct((1, 2 * rows + 8, 128), jnp.int32)
    imag = jax.ShapeDtypeStruct((1, 2 * rows, 128), jnp.int32)
    return pl.pallas_call(
        encode_kernel,
        out_shape=(real, imag, real, imag),
        in_specs=[pl.BlockSpec(memory_space=pltpu.SMEM), pl.BlockSpec(memory_space=pltpu.VMEM)],
        out_specs=(pl.BlockSpec(memory_space=pltpu.VMEM),) * 4,
        scratch_shapes=[pltpu.VMEM((2, rows, ROWS), jnp.float32)],
    )(core.reshape(1), strain)


def make_kernel(slots, real_masks, imag_masks):
    blocks = [len(masks) for masks in (real_masks, imag_masks)]

    def kernel(*refs):
        plan_ref, edge_ref, own_ref, mate_ref = refs[:4]
        real_refs = refs[4 : 4 + blocks[0]]
        imag_refs = refs[4 + blocks[0] : 4 + sum(blocks)]
        (first_ref, second_ref, octet_ref, rows_ref, base_ref, shift_ref, coarse_ref, lanes_ref, out_ref, strain_ref,
         wave_ref, between_ref, q_ref, p_ref, x_ref, o_ref, l_ref, z_ref, fold_ref, peak_ref, power_ref, sem) = refs[4 + sum(blocks) :]
        live = plan_ref[slots]
        own_count = plan_ref[slots + 1]
        device = plan_ref[slots + 2]

        def fetch(step):
            slot = plan_ref[step]
            buffer = step % 2

            @pl.when(step < own_count)
            def _():
                pltpu.make_async_copy(own_ref.at[slot], wave_ref.at[buffer], sem.at[buffer]).start()

            @pl.when(step >= own_count)
            def _():
                pltpu.make_async_copy(mate_ref.at[slot - slots // 2], wave_ref.at[buffer], sem.at[buffer]).start()

        fetch(0)
        out_ref[...] = jnp.zeros_like(out_ref)

        held = imag_refs[0].shape[1] // 2
        same = lax.broadcasted_iota(jnp.int32, (held, 128), 0) == lax.broadcasted_iota(jnp.int32, (held, 128), 1)
        for part, (part_refs, masks) in enumerate(((real_refs, real_masks), (imag_refs, imag_masks))):
            for ref, group in zip(part_refs, masks):
                for i, mask in enumerate(group):
                    row = pl.multiple_of((device ^ mask) * held, held)
                    if part == 0:
                        line = jnp.broadcast_to(ref[i, 2 * held : 2 * held + 1, :], (held, 128))
                        exponent = jnp.sum(jnp.where(same, line, 0).astype(jnp.float32), axis=1, keepdims=True)
                        scale = jnp.broadcast_to(jnp.exp2(exponent - 15.0), (held, 128))
                        strain_ref[2, pl.ds(row, held), 0:128] = scale
                    scale = strain_ref[2, pl.ds(row, held), 0:128]
                    for tile in range(2):
                        word = ref[i, tile * held : (tile + 1) * held, :]
                        high = (word >> 16).astype(jnp.float32) * scale
                        low = ((word << 16) >> 16).astype(jnp.float32) * scale
                        strain_ref[part, pl.ds(row, held), tile * 128 : tile * 128 + 128] = high
                        strain_ref[part, pl.ds(row, held), HALF + tile * 128 : HALF + tile * 128 + 128] = low

        for v in range(4):
            for mirror in range(2):
                at = mirror * 4 + v
                base_r = base_ref[0]
                base_i = base_ref[1] if mirror == 0 else -base_ref[1]
                shift_r = shift_ref[0, at : at + 1, :]
                shift_i = shift_ref[1, at : at + 1, :]
                between_ref[v, mirror, 0] = base_r * shift_r - base_i * shift_i
                between_ref[v, mirror, 1] = base_r * shift_i + base_i * shift_r

        def one_slot(step, carry):
            slot = plan_ref[step]
            buffer = step % 2
            base = slot * (BINS + 1)
            first_edge = edge_ref[base]
            last_edge = edge_ref[base + BINS]

            @pl.when(step + 1 < live)
            def _():
                fetch(step + 1)

            pltpu.make_async_copy(own_ref.at[0], wave_ref.at[buffer], sem.at[buffer]).wait()

            def trim(r):
                start = r * ROWS

                @pl.when((start < first_edge) | (start + 16 * ROWS > last_edge))
                def _():
                    index = lax.broadcasted_iota(jnp.int32, (16, ROWS), 0) * ROWS + lax.broadcasted_iota(
                        jnp.int32, (16, ROWS), 1
                    )
                    inside = (index >= first_edge - start) & (index < last_edge - start)
                    for part in range(2):
                        wave = wave_ref[buffer, part, pl.ds(r, 16), :].astype(jnp.float32)
                        wave_ref[buffer, part, pl.ds(r, 16), :] = jnp.where(inside, wave, 0.0).astype(jnp.bfloat16)

            def product(r, lane):
                data_r = strain_ref[0, pl.ds(r, 16), lane : lane + 128]
                data_i = strain_ref[1, pl.ds(r, 16), lane : lane + 128]
                wave_r = wave_ref[buffer, 0, pl.ds(r, 16), lane : lane + 128].astype(jnp.float32)
                wave_i = wave_ref[buffer, 1, pl.ds(r, 16), lane : lane + 128].astype(jnp.float32)
                real = data_r * wave_r + data_i * wave_i
                imag = data_i * wave_r - data_r * wave_i
                q_ref[0, pl.ds(r, 16), lane : lane + 128] = real
                q_ref[1, pl.ds(r, 16), lane : lane + 128] = imag
                p_ref[pl.ds(r, 16), lane : lane + 128] = wave_r * wave_r + wave_i * wave_i
                return real, imag

            def front(c, carry):
                r = pl.multiple_of(c * 16, 16)
                above = pl.multiple_of(r + HALF, 16)
                for lane in range(0, ROWS, 128):
                    low_r, low_i = product(r, lane)
                    high_r, high_i = product(above, lane)
                    mixed = [
                        (low_r + high_r, low_i + high_i),
                        (low_r - high_i, low_i + high_r),
                        (low_r - high_r, low_i - high_i),
                        (low_r + high_i, low_i - high_r),
                    ]
                    for v in range(4):
                        real, imag = mixed[v]
                        if v != 2:
                            at = (1, 0, 0, 0)[v]
                            cosine = rows_ref[at, 0, pl.ds(r, 16), :]
                            sine = rows_ref[at, 1, pl.ds(r, 16), :]
                            if v == 3:
                                real, imag = real * cosine - imag * sine, real * sine + imag * cosine
                            else:
                                real, imag = real * cosine + imag * sine, imag * cosine - real * sine
                        for part, value in ((0, real), (1, imag)):
                            high, low = split_bf16(value)
                            column = (2 * v + part) * ROWS + lane
                            x_ref[pl.ds(r, 16), column : column + 128] = high
                            x_ref[pl.ds(above, 16), column : column + 128] = low
                return carry

            def clear(c, carry):
                trim(pl.multiple_of(c * 16, 16))
                return carry

            lax.fori_loop(0, first_edge // (16 * ROWS) + 1, clear, 0)
            lax.fori_loop(last_edge // (16 * ROWS), ROWS // 16, clear, 0)
            lax.fori_loop(0, HALF // 16, front, 0, unroll=2)

            offset = lax.broadcasted_iota(jnp.int32, (8, ROWS), 0) * ROWS + lax.broadcasted_iota(
                jnp.int32, (8, ROWS), 1
            )
            for b in range(BINS):
                lower = edge_ref[base + b]
                upper = edge_ref[base + b + 1]

                def gather(i, carry, lower=lower, upper=upper):
                    real, imag, power = carry
                    r = pl.multiple_of(i * 8, 8)
                    start = i * (8 * ROWS)
                    mask = (offset >= lower - start) & (offset < upper - start)
                    real = real + jnp.where(mask, q_ref[0, pl.ds(r, 8), :], 0.0)
                    imag = imag + jnp.where(mask, q_ref[1, pl.ds(r, 8), :], 0.0)
                    power = power + jnp.where(mask, p_ref[pl.ds(r, 8), :], 0.0)
                    return real, imag, power

                zero = jnp.zeros((8, ROWS), jnp.float32)
                real, imag, power = lax.fori_loop(
                    lower // (8 * ROWS), (upper + (8 * ROWS - 1)) // (8 * ROWS), gather, (zero, zero, zero)
                )
                fold_ref[0:8, b * ROWS : (b + 1) * ROWS] = real
                fold_ref[8:16, b * ROWS : (b + 1) * ROWS] = imag
                power_ref[8 * b : 8 * b + 8, :] = (
                    power[:, :128] + power[:, 128:256] + power[:, 256:384] + power[:, 384:]
                )
            power = jnp.sum(jnp.sum(power_ref[...].reshape(BINS, 8, 128), axis=1), axis=1, keepdims=True)
            energy = jnp.sum(power, axis=0, keepdims=True)
            weight = jnp.broadcast_to(power / energy, (BINS, 128))
            inverse = jnp.broadcast_to(1.0 / (power + EPSILON), (BINS, 128))


            def rows_stage(v, j):
                column = v * 2 * ROWS + j * HALF
                o_ref[v % 2, :, j * HALF : (j + 1) * HALF] = jnp.dot(
                    first_ref[...],
                    jnp.concatenate([x_ref[:, column : column + HALF], x_ref[0:HALF, column : column + HALF]], axis=0),
                    preferred_element_type=jnp.float32,
                )

            def middle(v, chunk):
                u = chunk * CHUNK
                cos_r = o_ref[v % 2, u : u + CHUNK, :ROWS]
                cos_i = o_ref[v % 2, u : u + CHUNK, ROWS:]
                sin_r = o_ref[v % 2, QUART + u : QUART + u + CHUNK, :ROWS]
                sin_i = o_ref[v % 2, QUART + u : QUART + u + CHUNK, ROWS:]
                for mirror in range(2):
                    if mirror == 0:
                        real, imag = cos_r - sin_i, cos_i + sin_r
                    else:
                        real, imag = cos_r + sin_i, cos_i - sin_r
                    cosine = between_ref[v, mirror, 0, u : u + CHUNK, :]
                    sine = between_ref[v, mirror, 1, u : u + CHUNK, :]
                    real, imag = real * cosine - imag * sine, real * sine + imag * cosine
                    values = lane_butterfly(real, imag, lanes_ref[0, 0:1, :], lanes_ref[1, 0:1, :])
                    for part in range(4):
                        high, low = split_bf16(values[part])
                        at = ((chunk * 2 + mirror) * 4 + part) * CHUNK
                        l_ref[v % 2, at : at + CHUNK, :HALF] = high
                        l_ref[v % 2, at : at + CHUNK, HALF:] = low

            def columns_stage(v, chunk):
                at = chunk * 8 * CHUNK
                z_ref[v % 2, at : at + 8 * CHUNK, :] = jnp.dot(
                    jnp.concatenate(
                        [l_ref[v % 2, at : at + 8 * CHUNK, :], l_ref[v % 2, at : at + 8 * CHUNK, :HALF]], axis=1
                    ),
                    second_ref[...],
                    preferred_element_type=jnp.float32,
                )

            def finish(v, chunk):
                for mirror in range(2):
                    cell = chunk if mirror == 0 else 7 - chunk
                    for parity in range(2):
                        at = ((chunk * 2 + mirror) * 4 + parity * 2) * CHUNK
                        real = z_ref[v % 2, at : at + CHUNK, :]
                        imag = z_ref[v % 2, at + CHUNK : at + 2 * CHUNK, :]
                        a, d = real[:, :128], real[:, 128:]
                        c, e = imag[:, :128], imag[:, 128:]
                        for side in range(2):
                            if side == 0:
                                re, im = a - e, c + d
                            else:
                                re, im = a + e, c - d
                            square = re * re + im * im
                            best = jnp.max(square.reshape(CHUNK // 8, 8, 128), axis=0)
                            lane = (parity * 2 + side) * 128
                            if v:
                                best = jnp.maximum(best, peak_ref[cell, :, lane : lane + 128])
                            peak_ref[cell, :, lane : lane + 128] = best

            for turn in range(6):
                for j in range(4):
                    if turn < 4:
                        rows_stage(turn, j)
                    if 2 <= turn:
                        columns_stage(turn - 2, j)
                    if 1 <= turn < 5:
                        middle(turn - 1, j)
                    if 2 <= turn:
                        finish(turn - 2, j)

            coarse_r = jnp.concatenate([coarse_ref[0], coarse_ref[0]], axis=0)
            coarse_i = jnp.concatenate([coarse_ref[1], coarse_ref[1]], axis=0)
            for b in range(0, BINS, 2):
                high, low = split_bf16(fold_ref[:, b * ROWS : (b + 2) * ROWS])
                bands = jnp.dot(
                    octet_ref[...], jnp.concatenate([high, low, high], axis=0), preferred_element_type=jnp.float32
                )
                real = jnp.concatenate([bands[0:8, :ROWS], bands[0:8, ROWS:]], axis=0)
                imag = jnp.concatenate([bands[8:16, :ROWS], bands[8:16, ROWS:]], axis=0)
                real, imag = real * coarse_r - imag * coarse_i, real * coarse_i + imag * coarse_r
                values = lane_butterfly(real, imag, lanes_ref[0, 0:1, :], lanes_ref[1, 0:1, :])
                for part in range(4):
                    high, low = split_bf16(values[part])
                    at = part * 128 + b * 8
                    l_ref[0, at : at + 16, :HALF] = high
                    l_ref[0, at : at + 16, HALF:] = low
            z_ref[0, 0:512, :] = jnp.dot(
                jnp.concatenate([l_ref[0, 0:512, :], l_ref[0, 0:512, :HALF]], axis=1),
                second_ref[...],
                preferred_element_type=jnp.float32,
            )
            loud = jnp.concatenate(
                [jnp.max(peak_ref[cell], axis=0, keepdims=True) for cell in range(8)], axis=0
            )
            top = jnp.zeros((8, 128), jnp.float32)
            for parity in range(2):
                real = z_ref[0, parity * 256 : parity * 256 + 128, :]
                imag = z_ref[0, parity * 256 + 128 : parity * 256 + 256, :]
                a, d = real[:, :128], real[:, 128:]
                c, e = imag[:, :128], imag[:, 128:]
                for side in range(2):
                    if side == 0:
                        re, im = a - e, c + d
                    else:
                        re, im = a + e, c - d
                    re = re.reshape(BINS, 8, 128)
                    im = im.reshape(BINS, 8, 128)
                    total_r = jnp.sum(re, axis=0)
                    total_i = jnp.sum(im, axis=0)
                    misfit = jnp.zeros((8, 128), jnp.float32)
                    for b in range(BINS):
                        error_r = re[b] - weight[b : b + 1] * total_r
                        error_i = im[b] - weight[b : b + 1] * total_i
                        misfit = misfit + (error_r * error_r + error_i * error_i) * inverse[b : b + 1]
                    reduced = misfit / (2 * BINS - 2)
                    factor = jnp.where(
                        reduced > 1.0, jnp.exp(jnp.log((1.0 + reduced * reduced * reduced) / 2.0) * (-1.0 / 6.0)), 1.0
                    )
                    lane = (parity * 2 + side) * 128
                    top = jnp.maximum(top, jnp.sqrt(loud[:, lane : lane + 128]) * factor)
            best = jnp.max(top, axis=(0, 1), keepdims=True) / jnp.sqrt(energy)
            out_ref[pl.ds(slot, 1), :] = jnp.broadcast_to(best, (1, 128))
            return carry

        lax.fori_loop(0, live, one_slot, 0)

    return kernel


def slot_peaks(plan, edges, own_waves, mate_waves, real_blocks, imag_blocks, real_masks, imag_masks):
    slots = 2 * own_waves.shape[0]
    tables = [jnp.asarray(table) for table in host_tables()]
    smem = pl.BlockSpec(memory_space=pltpu.SMEM)
    hbm = pl.BlockSpec(memory_space=pl.ANY)
    vmem = pl.BlockSpec(memory_space=pltpu.VMEM)
    return pl.pallas_call(
        make_kernel(slots, real_masks, imag_masks),
        out_shape=jax.ShapeDtypeStruct((slots, 128), jnp.float32),
        in_specs=[smem, smem, hbm, hbm] + [vmem] * (len(real_blocks) + len(imag_blocks) + len(tables)),
        out_specs=vmem,
        scratch_shapes=[
            pltpu.VMEM((3, ROWS, ROWS), jnp.float32),
            pltpu.VMEM((2, 2, ROWS, ROWS), jnp.bfloat16),
            pltpu.VMEM((4, 2, 2, QUART, ROWS), jnp.float32),
            pltpu.VMEM((2, ROWS, ROWS), jnp.float32),
            pltpu.VMEM((ROWS, ROWS), jnp.float32),
            pltpu.VMEM((ROWS, 8 * ROWS), jnp.bfloat16),
            pltpu.VMEM((2, HALF, 2 * ROWS), jnp.float32),
            pltpu.VMEM((2, 1024, ROWS), jnp.bfloat16),
            pltpu.VMEM((2, 1024, HALF), jnp.float32),
            pltpu.VMEM((16, BINS * ROWS), jnp.float32),
            pltpu.VMEM((8, 8, ROWS), jnp.float32),
            pltpu.VMEM((8 * BINS, 128), jnp.float32),
            pltpu.SemaphoreType.DMA((2,)),
        ],
        compiler_params=pltpu.CompilerParams(vmem_limit_bytes=48 << 20),
    )(plan, edges, own_waves, mate_waves, *real_blocks, *imag_blocks, *tables)


def exchange(x, bit):
    devices = lax.axis_size("bank")
    return lax.ppermute(x, "bank", [(i, i ^ bit) for i in range(devices)])


def per_device(strain, templates, counts, edges):
    devices = lax.axis_size("bank")
    device = lax.axis_index("bank").astype(jnp.int32)
    core = device % 2
    slots = templates.shape[0]
    bits = [1 << i for i in range(1, devices.bit_length() - 1)]
    orders = [bits[::-1], bits[:1] + bits[:0:-1]]

    own_real, own_imag, other_real, other_imag = encode(core, strain)
    current = [
        jnp.concatenate([own, exchange(other, 1)]) for own, other in ((own_real, other_real), (own_imag, other_imag))
    ]
    small = jnp.concatenate([counts, edges.reshape(-1)])
    mate_small = exchange(small, 1)
    templates, mate_small, *current = lax.optimization_barrier((templates, mate_small, *current))
    own_waves = templates.reshape(slots, 2, ROWS, ROWS)
    masks = [[0, 1], [0, 1]]
    for level in range(len(bits)):
        arrived = [exchange(current[half], orders[half][level]) for half in range(2)]
        added = [[m ^ orders[half][level] for m in masks[half]] for half in range(2)]
        if level + 1 < len(bits):
            current = [jnp.concatenate([current[half], arrived[half]]) for half in range(2)]
            masks = [masks[half] + added[half] for half in range(2)]
        if level + 2 == len(bits):
            own_waves, *current = lax.optimization_barrier((own_waves, *current))
            mate_waves = exchange(own_waves, 1)
    blocks = [[current[half], arrived[half]] for half in range(2)]
    block_masks = [[masks[half], added[half]] for half in range(2)]

    own_count = small[0]
    live = own_count + mate_small[0]
    ramp = jnp.minimum(jnp.arange(2 * slots, dtype=jnp.int32), live - 1)
    order = jnp.where(ramp < own_count, ramp, slots + ramp - own_count)
    plan = jnp.concatenate([order, live[None], own_count[None], device[None]]).astype(jnp.int32)
    all_edges = jnp.concatenate([small[1:], mate_small[1:]])
    peaks = slot_peaks(plan, all_edges, own_waves, mate_waves, *blocks, *block_masks)

    mine = lax.broadcasted_iota(jnp.int32, peaks.shape, 1) % 2 == core
    arrived = exchange(peaks, 1)
    swapped = jnp.concatenate([arrived[slots:], arrived[:slots]])
    both = jnp.where(mine, peaks, swapped)
    best = both
    for bit in bits:
        best = jnp.maximum(best, exchange(best, bit))
    return (both[:slots, :2], jnp.max(best, axis=0)[:2])


def solution(mesh):
    placed = (P("seg", None, "bank"), P("bank", None, None), P("bank"), P("bank", None))
    return jax.shard_map(
        per_device,
        mesh=mesh,
        in_specs=placed,
        out_specs=(P("bank", "seg"), P("seg")),
        check_vma=False,
    )
```

```python
import numpy as np

import jax
import jax.numpy as jnp
from jax import lax
from jax.experimental import pallas as pl
from jax.experimental.pallas import tpu as pltpu
from jax.sharding import PartitionSpec as P

CELL = 128
BINS = 16
EPSILON = 1e-06
ROWS = 512
HALF = 256
QUART = 128
CHUNK = 32


def split_bf16(x):
    high = x.astype(jnp.bfloat16)
    low = (x - high.astype(jnp.float32)).astype(jnp.bfloat16)
    return high, low


def host_split(x):
    high = x.astype(np.float32).astype(jnp.bfloat16)
    low = (x - high.astype(np.float64)).astype(np.float32).astype(jnp.bfloat16)
    return high, low


def host_tables():
    k = np.arange(HALF)
    u = np.arange(QUART) + 0.5
    angle = 2 * np.pi * u[:, None] * k[None, :] / HALF
    wave = np.concatenate([np.cos(angle), np.sin(angle)], axis=0)
    high, low = host_split(wave)
    first = np.concatenate([high, high, low], axis=1)
    second = np.concatenate([high.T, high.T, low.T], axis=0)
    eight = 2 * np.pi * (np.arange(8)[:, None] * np.arange(8)[None, :] % 8) / 8
    block = np.block([[np.cos(eight), -np.sin(eight)], [np.sin(eight), np.cos(eight)]])
    high, low = host_split(block)
    octet = np.concatenate([high, high, low], axis=1)
    angle = 2 * np.pi * k[None, :] * np.array([1, 2])[:, None] / 1024
    rows = np.stack([np.cos(angle), np.sin(angle)], axis=1)
    rows = np.broadcast_to(rows[..., None], rows.shape + (128,)).astype(np.float32)
    unit = 2 * np.pi / (1 << 19)
    angle = unit * (4 * np.arange(QUART)[:, None] * np.arange(ROWS))
    between = np.stack([np.cos(angle), np.sin(angle)]).astype(np.float32)
    angle = unit * (np.array([0, 1, 2, 3, 1020, 1021, 1022, 1023])[:, None] * np.arange(ROWS))
    shift = np.stack([np.cos(angle), np.sin(angle)]).astype(np.float32)
    angle = unit * (128 * np.arange(8)[:, None] * np.arange(ROWS)[None, :])
    coarse = np.stack([np.cos(angle), np.sin(angle)]).astype(np.float32)
    angle = -2 * np.pi * k / ROWS
    lanes = np.stack([np.cos(angle), np.sin(angle)]).astype(np.float32)
    lanes = np.broadcast_to(lanes[:, None, :], (2, 8, HALF)).copy()
    return first, second, octet, rows.copy(), between, shift, coarse, lanes


def lane_butterfly(real, imag, lanes_real, lanes_imag):
    low_r, high_r = real[:, :HALF], real[:, HALF:]
    low_i, high_i = imag[:, :HALF], imag[:, HALF:]
    sum_r, sum_i = low_r + high_r, low_i + high_i
    even_r = sum_r * lanes_real - sum_i * lanes_imag
    even_i = sum_r * lanes_imag + sum_i * lanes_real
    return even_r, even_i, low_r - high_r, low_i - high_i


def encode_kernel(core_ref, strain_ref, own_real_ref, own_imag_ref, other_real_ref, other_imag_ref, rows_ref):
    rows = rows_ref.shape[1]
    for which, out_refs in enumerate(((own_real_ref, own_imag_ref), (other_real_ref, other_imag_ref))):
        segment = core_ref[0] if which == 0 else 1 - core_ref[0]
        for part in range(2):
            for row in range(rows):
                rows_ref[part, row : row + 1, :] = strain_ref[segment, part : part + 1, row * ROWS : (row + 1) * ROWS]
        data = [rows_ref[0], rows_ref[1]]
        largest = jnp.max(jnp.maximum(jnp.abs(data[0]), jnp.abs(data[1])), axis=1, keepdims=True)
        exponent = jnp.floor(jnp.log2(jnp.maximum(largest, 1e-30)) + 1.001)
        scale = jnp.exp2(15.0 - exponent)
        for value, out_ref in zip(data, out_refs):
            number = jnp.clip(jnp.round(value * scale), -32767.0, 32767.0).astype(jnp.int32)
            packed = (number[:, :HALF] << 16) | (number[:, HALF:] & 0xFFFF)
            out_ref[0, 0:rows, :] = packed[:, :128]
            out_ref[0, rows : 2 * rows, :] = packed[:, 128:]
        spread = jnp.broadcast_to(exponent.astype(jnp.int32), (rows, 128))
        same = lax.broadcasted_iota(jnp.int32, (rows, 128), 0) == lax.broadcasted_iota(jnp.int32, (rows, 128), 1)
        line = jnp.sum(jnp.where(same, spread, 0), axis=0, keepdims=True)
        out_refs[0][0, 2 * rows :, :] = jnp.broadcast_to(line, (8, 128))


def encode(core, strain):
    rows = strain.shape[2] // ROWS
    real = jax.ShapeDtypeStruct((1, 2 * rows + 8, 128), jnp.int32)
    imag = jax.ShapeDtypeStruct((1, 2 * rows, 128), jnp.int32)
    return pl.pallas_call(
        encode_kernel,
        out_shape=(real, imag, real, imag),
        in_specs=[pl.BlockSpec(memory_space=pltpu.SMEM), pl.BlockSpec(memory_space=pltpu.VMEM)],
        out_specs=(pl.BlockSpec(memory_space=pltpu.VMEM),) * 4,
        scratch_shapes=[pltpu.VMEM((2, rows, ROWS), jnp.float32)],
    )(core.reshape(1), strain)


def make_kernel(slots, real_masks, imag_masks):
    blocks = [len(masks) for masks in (real_masks, imag_masks)]

    def kernel(*refs):
        plan_ref, edge_ref, own_ref, mate_ref = refs[:4]
        real_refs = refs[4 : 4 + blocks[0]]
        imag_refs = refs[4 + blocks[0] : 4 + sum(blocks)]
        (first_ref, second_ref, octet_ref, rows_ref, base_ref, shift_ref, coarse_ref, lanes_ref, out_ref, strain_ref,
         wave_ref, between_ref, qa_ref, qb_ref, pa_ref, pb_ref, xa_ref, xb_ref, o_ref, l_ref, z_ref, fold_ref, peak_ref, power_ref, sem) = refs[4 + sum(blocks) :]
        q_refs, p_refs, x_refs = (qa_ref, qb_ref), (pa_ref, pb_ref), (xa_ref, xb_ref)
        live = plan_ref[slots]
        own_count = plan_ref[slots + 1]
        device = plan_ref[slots + 2]

        def fetch(step):
            slot = plan_ref[step]
            buffer = step % 2

            @pl.when(step < own_count)
            def _():
                pltpu.make_async_copy(own_ref.at[slot], wave_ref.at[buffer], sem.at[buffer]).start()

            @pl.when(step >= own_count)
            def _():
                pltpu.make_async_copy(mate_ref.at[slot - slots // 2], wave_ref.at[buffer], sem.at[buffer]).start()

        fetch(0)
        out_ref[...] = jnp.zeros_like(out_ref)

        held = imag_refs[0].shape[1] // 2
        same = lax.broadcasted_iota(jnp.int32, (held, 128), 0) == lax.broadcasted_iota(jnp.int32, (held, 128), 1)
        for part, (part_refs, masks) in enumerate(((real_refs, real_masks), (imag_refs, imag_masks))):
            for ref, group in zip(part_refs, masks):
                for i, mask in enumerate(group):
                    row = pl.multiple_of((device ^ mask) * held, held)
                    if part == 0:
                        line = jnp.broadcast_to(ref[i, 2 * held : 2 * held + 1, :], (held, 128))
                        exponent = jnp.sum(jnp.where(same, line, 0).astype(jnp.float32), axis=1, keepdims=True)
                        scale = jnp.broadcast_to(jnp.exp2(exponent - 15.0), (held, 128))
                        strain_ref[2, pl.ds(row, held), 0:128] = scale
                    scale = strain_ref[2, pl.ds(row, held), 0:128]
                    for tile in range(2):
                        word = ref[i, tile * held : (tile + 1) * held, :]
                        high = (word >> 16).astype(jnp.float32) * scale
                        low = ((word << 16) >> 16).astype(jnp.float32) * scale
                        strain_ref[part, pl.ds(row, held), tile * 128 : tile * 128 + 128] = high
                        strain_ref[part, pl.ds(row, held), HALF + tile * 128 : HALF + tile * 128 + 128] = low

        for v in range(4):
            for mirror in range(2):
                at = mirror * 4 + v
                base_r = base_ref[0]
                base_i = base_ref[1] if mirror == 0 else -base_ref[1]
                shift_r = shift_ref[0, at : at + 1, :]
                shift_i = shift_ref[1, at : at + 1, :]
                between_ref[v, mirror, 0] = base_r * shift_r - base_i * shift_i
                between_ref[v, mirror, 1] = base_r * shift_i + base_i * shift_r

        def edges_of(step):
            base = plan_ref[step] * (BINS + 1)
            return edge_ref[base], edge_ref[base + BINS]

        def arrive(step, buffer):
            pltpu.make_async_copy(own_ref.at[0], wave_ref.at[buffer], sem.at[buffer]).wait()
            first_edge, last_edge = edges_of(step)

            def trim(r):
                start = r * ROWS

                @pl.when((start < first_edge) | (start + 16 * ROWS > last_edge))
                def _():
                    index = lax.broadcasted_iota(jnp.int32, (16, ROWS), 0) * ROWS + lax.broadcasted_iota(
                        jnp.int32, (16, ROWS), 1
                    )
                    inside = (index >= first_edge - start) & (index < last_edge - start)
                    for part in range(2):
                        wave = wave_ref[buffer, part, pl.ds(r, 16), :].astype(jnp.float32)
                        wave_ref[buffer, part, pl.ds(r, 16), :] = jnp.where(inside, wave, 0.0).astype(jnp.bfloat16)

            def clear(c, carry):
                trim(pl.multiple_of(c * 16, 16))
                return carry

            lax.fori_loop(0, first_edge // (16 * ROWS) + 1, clear, 0)
            lax.fori_loop(last_edge // (16 * ROWS), ROWS // 16, clear, 0)

        def front(c, buffer):
            q_ref, p_ref, x_ref = q_refs[buffer], p_refs[buffer], x_refs[buffer]

            def product(r, lane):
                data_r = strain_ref[0, pl.ds(r, 16), lane : lane + 128]
                data_i = strain_ref[1, pl.ds(r, 16), lane : lane + 128]
                wave_r = wave_ref[buffer, 0, pl.ds(r, 16), lane : lane + 128].astype(jnp.float32)
                wave_i = wave_ref[buffer, 1, pl.ds(r, 16), lane : lane + 128].astype(jnp.float32)
                real = data_r * wave_r + data_i * wave_i
                imag = data_i * wave_r - data_r * wave_i
                q_ref[0, pl.ds(r, 16), lane : lane + 128] = real
                q_ref[1, pl.ds(r, 16), lane : lane + 128] = imag
                p_ref[pl.ds(r, 16), lane : lane + 128] = wave_r * wave_r + wave_i * wave_i
                return real, imag

            r = c * 16 if isinstance(c, int) else pl.multiple_of(c * 16, 16)
            above = r + HALF if isinstance(c, int) else pl.multiple_of(r + HALF, 16)
            for lane in range(0, ROWS, 128):
                low_r, low_i = product(r, lane)
                high_r, high_i = product(above, lane)
                mixed = [
                    (low_r + high_r, low_i + high_i),
                    (low_r - high_i, low_i + high_r),
                    (low_r - high_r, low_i - high_i),
                    (low_r + high_i, low_i - high_r),
                ]
                for v in range(4):
                    real, imag = mixed[v]
                    if v != 2:
                        at = (1, 0, 0, 0)[v]
                        cosine = rows_ref[at, 0, pl.ds(r, 16), :]
                        sine = rows_ref[at, 1, pl.ds(r, 16), :]
                        if v == 3:
                            real, imag = real * cosine - imag * sine, real * sine + imag * cosine
                        else:
                            real, imag = real * cosine + imag * sine, imag * cosine - real * sine
                    for part, value in ((0, real), (1, imag)):
                        high, low = split_bf16(value)
                        column = (2 * v + part) * ROWS + lane
                        x_ref[pl.ds(r, 16), column : column + 128] = high
                        x_ref[pl.ds(above, 16), column : column + 128] = low

        arrive(0, 0)

        @pl.when(live > 1)
        def _():
            fetch(1)

        def first_front(c, carry):
            front(c, 0)
            return carry

        lax.fori_loop(0, HALF // 16, first_front, 0)

        def one_slot(step, buffer):
            q_ref, p_ref, x_ref = q_refs[buffer], p_refs[buffer], x_refs[buffer]
            slot = plan_ref[step]
            base = slot * (BINS + 1)

            @pl.when(step + 1 < live)
            def _():
                arrive(step + 1, 1 - buffer)

            @pl.when(step + 2 < live)
            def _():
                fetch(step + 2)

            offset = lax.broadcasted_iota(jnp.int32, (8, ROWS), 0) * ROWS + lax.broadcasted_iota(
                jnp.int32, (8, ROWS), 1
            )
            for b in range(BINS):
                lower = edge_ref[base + b]
                upper = edge_ref[base + b + 1]

                def gather(i, carry, lower=lower, upper=upper):
                    real, imag, power = carry
                    r = pl.multiple_of(i * 8, 8)
                    start = i * (8 * ROWS)
                    mask = (offset >= lower - start) & (offset < upper - start)
                    real = real + jnp.where(mask, q_ref[0, pl.ds(r, 8), :], 0.0)
                    imag = imag + jnp.where(mask, q_ref[1, pl.ds(r, 8), :], 0.0)
                    power = power + jnp.where(mask, p_ref[pl.ds(r, 8), :], 0.0)
                    return real, imag, power

                zero = jnp.zeros((8, ROWS), jnp.float32)
                real, imag, power = lax.fori_loop(
                    lower // (8 * ROWS), (upper + (8 * ROWS - 1)) // (8 * ROWS), gather, (zero, zero, zero)
                )
                fold_ref[0:8, b * ROWS : (b + 1) * ROWS] = real
                fold_ref[8:16, b * ROWS : (b + 1) * ROWS] = imag
                power_ref[8 * b : 8 * b + 8, :] = (
                    power[:, :128] + power[:, 128:256] + power[:, 256:384] + power[:, 384:]
                )
            power = jnp.sum(jnp.sum(power_ref[...].reshape(BINS, 8, 128), axis=1), axis=1, keepdims=True)
            energy = jnp.sum(power, axis=0, keepdims=True)
            weight = jnp.broadcast_to(power / energy, (BINS, 128))
            inverse = jnp.broadcast_to(1.0 / (power + EPSILON), (BINS, 128))


            def rows_stage(v, j):
                column = v * 2 * ROWS + j * HALF
                o_ref[v % 2, :, j * HALF : (j + 1) * HALF] = jnp.dot(
                    first_ref[...],
                    jnp.concatenate([x_ref[:, column : column + HALF], x_ref[0:HALF, column : column + HALF]], axis=0),
                    preferred_element_type=jnp.float32,
                )

            def middle(v, chunk):
                u = chunk * CHUNK
                cos_r = o_ref[v % 2, u : u + CHUNK, :ROWS]
                cos_i = o_ref[v % 2, u : u + CHUNK, ROWS:]
                sin_r = o_ref[v % 2, QUART + u : QUART + u + CHUNK, :ROWS]
                sin_i = o_ref[v % 2, QUART + u : QUART + u + CHUNK, ROWS:]
                for mirror in range(2):
                    if mirror == 0:
                        real, imag = cos_r - sin_i, cos_i + sin_r
                    else:
                        real, imag = cos_r + sin_i, cos_i - sin_r
                    cosine = between_ref[v, mirror, 0, u : u + CHUNK, :]
                    sine = between_ref[v, mirror, 1, u : u + CHUNK, :]
                    real, imag = real * cosine - imag * sine, real * sine + imag * cosine
                    values = lane_butterfly(real, imag, lanes_ref[0, 0:1, :], lanes_ref[1, 0:1, :])
                    for part in range(4):
                        high, low = split_bf16(values[part])
                        at = ((chunk * 2 + mirror) * 4 + part) * CHUNK
                        l_ref[v % 2, at : at + CHUNK, :HALF] = high
                        l_ref[v % 2, at : at + CHUNK, HALF:] = low

            def columns_stage(v, chunk):
                at = chunk * 8 * CHUNK
                z_ref[v % 2, at : at + 8 * CHUNK, :] = jnp.dot(
                    jnp.concatenate(
                        [l_ref[v % 2, at : at + 8 * CHUNK, :], l_ref[v % 2, at : at + 8 * CHUNK, :HALF]], axis=1
                    ),
                    second_ref[...],
                    preferred_element_type=jnp.float32,
                )

            def finish(v, chunk):
                for mirror in range(2):
                    cell = chunk if mirror == 0 else 7 - chunk
                    for parity in range(2):
                        at = ((chunk * 2 + mirror) * 4 + parity * 2) * CHUNK
                        real = z_ref[v % 2, at : at + CHUNK, :]
                        imag = z_ref[v % 2, at + CHUNK : at + 2 * CHUNK, :]
                        a, d = real[:, :128], real[:, 128:]
                        c, e = imag[:, :128], imag[:, 128:]
                        for side in range(2):
                            if side == 0:
                                re, im = a - e, c + d
                            else:
                                re, im = a + e, c - d
                            square = re * re + im * im
                            best = jnp.max(square.reshape(CHUNK // 8, 8, 128), axis=0)
                            lane = (parity * 2 + side) * 128
                            if v:
                                best = jnp.maximum(best, peak_ref[cell, :, lane : lane + 128])
                            peak_ref[cell, :, lane : lane + 128] = best

            chunks = list(range(HALF // 16))
            for turn in range(6):
                for j in range(4):
                    if chunks:
                        front(chunks.pop(0), 1 - buffer)
                    if 1 <= turn < 5:
                        middle(turn - 1, j)
                    if turn < 4:
                        rows_stage(turn, j)
                    if 2 <= turn:
                        columns_stage(turn - 2, j)
                    if 2 <= turn:
                        finish(turn - 2, j)

            coarse_r = jnp.concatenate([coarse_ref[0], coarse_ref[0]], axis=0)
            coarse_i = jnp.concatenate([coarse_ref[1], coarse_ref[1]], axis=0)
            for b in range(0, BINS, 2):
                high, low = split_bf16(fold_ref[:, b * ROWS : (b + 2) * ROWS])
                bands = jnp.dot(
                    octet_ref[...], jnp.concatenate([high, low, high], axis=0), preferred_element_type=jnp.float32
                )
                real = jnp.concatenate([bands[0:8, :ROWS], bands[0:8, ROWS:]], axis=0)
                imag = jnp.concatenate([bands[8:16, :ROWS], bands[8:16, ROWS:]], axis=0)
                real, imag = real * coarse_r - imag * coarse_i, real * coarse_i + imag * coarse_r
                values = lane_butterfly(real, imag, lanes_ref[0, 0:1, :], lanes_ref[1, 0:1, :])
                for part in range(4):
                    high, low = split_bf16(values[part])
                    at = part * 128 + b * 8
                    l_ref[0, at : at + 16, :HALF] = high
                    l_ref[0, at : at + 16, HALF:] = low
            z_ref[0, 0:512, :] = jnp.dot(
                jnp.concatenate([l_ref[0, 0:512, :], l_ref[0, 0:512, :HALF]], axis=1),
                second_ref[...],
                preferred_element_type=jnp.float32,
            )
            loud = jnp.concatenate(
                [jnp.max(peak_ref[cell], axis=0, keepdims=True) for cell in range(8)], axis=0
            )
            top = jnp.zeros((8, 128), jnp.float32)
            for parity in range(2):
                real = z_ref[0, parity * 256 : parity * 256 + 128, :]
                imag = z_ref[0, parity * 256 + 128 : parity * 256 + 256, :]
                a, d = real[:, :128], real[:, 128:]
                c, e = imag[:, :128], imag[:, 128:]
                for side in range(2):
                    if side == 0:
                        re, im = a - e, c + d
                    else:
                        re, im = a + e, c - d
                    re = re.reshape(BINS, 8, 128)
                    im = im.reshape(BINS, 8, 128)
                    total_r = jnp.sum(re, axis=0)
                    total_i = jnp.sum(im, axis=0)
                    misfit = jnp.zeros((8, 128), jnp.float32)
                    for b in range(BINS):
                        error_r = re[b] - weight[b : b + 1] * total_r
                        error_i = im[b] - weight[b : b + 1] * total_i
                        misfit = misfit + (error_r * error_r + error_i * error_i) * inverse[b : b + 1]
                    reduced = misfit / (2 * BINS - 2)
                    factor = jnp.where(
                        reduced > 1.0, jnp.exp(jnp.log((1.0 + reduced * reduced * reduced) / 2.0) * (-1.0 / 6.0)), 1.0
                    )
                    lane = (parity * 2 + side) * 128
                    top = jnp.maximum(top, jnp.sqrt(loud[:, lane : lane + 128]) * factor)
            best = jnp.max(top, axis=(0, 1), keepdims=True) / jnp.sqrt(energy)
            out_ref[pl.ds(slot, 1), :] = jnp.broadcast_to(best, (1, 128))

        def pair(i, carry):
            one_slot(2 * i, 0)

            @pl.when(2 * i + 1 < live)
            def _():
                one_slot(2 * i + 1, 1)

            return carry

        lax.fori_loop(0, (live + 1) // 2, pair, 0)

    return kernel


def slot_peaks(plan, edges, own_waves, mate_waves, real_blocks, imag_blocks, real_masks, imag_masks):
    slots = 2 * own_waves.shape[0]
    tables = [jnp.asarray(table) for table in host_tables()]
    smem = pl.BlockSpec(memory_space=pltpu.SMEM)
    hbm = pl.BlockSpec(memory_space=pl.ANY)
    vmem = pl.BlockSpec(memory_space=pltpu.VMEM)
    return pl.pallas_call(
        make_kernel(slots, real_masks, imag_masks),
        out_shape=jax.ShapeDtypeStruct((slots, 128), jnp.float32),
        in_specs=[smem, smem, hbm, hbm] + [vmem] * (len(real_blocks) + len(imag_blocks) + len(tables)),
        out_specs=vmem,
        scratch_shapes=[
            pltpu.VMEM((3, ROWS, ROWS), jnp.float32),
            pltpu.VMEM((2, 2, ROWS, ROWS), jnp.bfloat16),
            pltpu.VMEM((4, 2, 2, QUART, ROWS), jnp.float32),
            pltpu.VMEM((2, ROWS, ROWS), jnp.float32),
            pltpu.VMEM((2, ROWS, ROWS), jnp.float32),
            pltpu.VMEM((ROWS, ROWS), jnp.float32),
            pltpu.VMEM((ROWS, ROWS), jnp.float32),
            pltpu.VMEM((ROWS, 8 * ROWS), jnp.bfloat16),
            pltpu.VMEM((ROWS, 8 * ROWS), jnp.bfloat16),
            pltpu.VMEM((2, HALF, 2 * ROWS), jnp.float32),
            pltpu.VMEM((2, 1024, ROWS), jnp.bfloat16),
            pltpu.VMEM((2, 1024, HALF), jnp.float32),
            pltpu.VMEM((16, BINS * ROWS), jnp.float32),
            pltpu.VMEM((8, 8, ROWS), jnp.float32),
            pltpu.VMEM((8 * BINS, 128), jnp.float32),
            pltpu.SemaphoreType.DMA((2,)),
        ],
        compiler_params=pltpu.CompilerParams(vmem_limit_bytes=48 << 20),
    )(plan, edges, own_waves, mate_waves, *real_blocks, *imag_blocks, *tables)


def exchange(x, bit):
    devices = lax.axis_size("bank")
    return lax.ppermute(x, "bank", [(i, i ^ bit) for i in range(devices)])


def per_device(strain, templates, counts, edges):
    devices = lax.axis_size("bank")
    device = lax.axis_index("bank").astype(jnp.int32)
    core = device % 2
    slots = templates.shape[0]
    bits = [1 << i for i in range(1, devices.bit_length() - 1)]
    orders = [bits[::-1], bits[:1] + bits[:0:-1]]

    own_real, own_imag, other_real, other_imag = encode(core, strain)
    current = [
        jnp.concatenate([own, exchange(other, 1)]) for own, other in ((own_real, other_real), (own_imag, other_imag))
    ]
    templates, edges, *current = lax.optimization_barrier((templates, edges, *current))
    small = jnp.concatenate([counts, edges.reshape(-1)])
    mate_small = exchange(small, 1)
    own_waves = templates.reshape(slots, 2, ROWS, ROWS)
    masks = [[0, 1], [0, 1]]
    for level in range(len(bits)):
        arrived = [exchange(current[half], orders[half][level]) for half in range(2)]
        added = [[m ^ orders[half][level] for m in masks[half]] for half in range(2)]
        if level + 1 < len(bits):
            current = [jnp.concatenate([current[half], arrived[half]]) for half in range(2)]
            masks = [masks[half] + added[half] for half in range(2)]
        if level + 2 == len(bits):
            own_waves, mate_small, *current = lax.optimization_barrier((own_waves, mate_small, *current))
            mate_waves = exchange(own_waves, 1)
    blocks = [[current[half], arrived[half]] for half in range(2)]
    block_masks = [[masks[half], added[half]] for half in range(2)]

    own_count = small[0]
    live = own_count + mate_small[0]
    ramp = jnp.minimum(jnp.arange(2 * slots, dtype=jnp.int32), live - 1)
    order = jnp.where(ramp < own_count, ramp, slots + ramp - own_count)
    plan = jnp.concatenate([order, live[None], own_count[None], device[None]]).astype(jnp.int32)
    all_edges = jnp.concatenate([small[1:], mate_small[1:]])
    peaks = slot_peaks(plan, all_edges, own_waves, mate_waves, *blocks, *block_masks)

    mine = lax.broadcasted_iota(jnp.int32, peaks.shape, 1) % 2 == core
    arrived = exchange(peaks, 1)
    swapped = jnp.concatenate([arrived[slots:], arrived[:slots]])
    both = jnp.where(mine, peaks, swapped)
    best = both
    for bit in bits:
        best = jnp.maximum(best, exchange(best, bit))
    return (both[:slots, :2], jnp.max(best, axis=0)[:2])


def solution(mesh):
    placed = (P("seg", None, "bank"), P("bank", None, None), P("bank"), P("bank", None))
    return jax.shard_map(
        per_device,
        mesh=mesh,
        in_specs=placed,
        out_specs=(P("bank", "seg"), P("seg")),
        check_vma=False,
    )
```

```python
import numpy as np

import jax
import jax.numpy as jnp
from jax import lax
from jax.experimental import pallas as pl
from jax.experimental.pallas import tpu as pltpu
from jax.sharding import PartitionSpec as P

CELL = 128
BINS = 16
EPSILON = 1e-06
ROWS = 512
HALF = 256
QUART = 128
CHUNK = 32


def split_bf16(x):
    high = x.astype(jnp.bfloat16)
    low = (x - high.astype(jnp.float32)).astype(jnp.bfloat16)
    return high, low


def host_split(x):
    high = x.astype(np.float32).astype(jnp.bfloat16)
    low = (x - high.astype(np.float64)).astype(np.float32).astype(jnp.bfloat16)
    return high, low


def host_tables():
    k = np.arange(HALF)
    u = np.arange(QUART) + 0.5
    angle = 2 * np.pi * u[:, None] * k[None, :] / HALF
    wave = np.concatenate([np.cos(angle), np.sin(angle)], axis=0)
    high, low = host_split(wave)
    first = np.concatenate([high, high, low], axis=1)
    second = np.concatenate([high.T, high.T, low.T], axis=0)
    eight = 2 * np.pi * (np.arange(8)[:, None] * np.arange(8)[None, :] % 8) / 8
    block = np.block([[np.cos(eight), -np.sin(eight)], [np.sin(eight), np.cos(eight)]])
    high, low = host_split(block)
    octet = np.concatenate([high, high, low], axis=1)
    angle = 2 * np.pi * k[None, :] * np.array([1, 2])[:, None] / 1024
    rows = np.stack([np.cos(angle), np.sin(angle)], axis=1)
    rows = np.broadcast_to(rows[..., None], rows.shape + (128,)).astype(np.float32)
    unit = 2 * np.pi / (1 << 19)
    angle = unit * (4 * np.arange(QUART)[:, None] * np.arange(ROWS))
    between = np.stack([np.cos(angle), np.sin(angle)]).astype(np.float32)
    angle = unit * (np.array([0, 1, 2, 3, 1020, 1021, 1022, 1023])[:, None] * np.arange(ROWS))
    shift = np.stack([np.cos(angle), np.sin(angle)]).astype(np.float32)
    angle = unit * (128 * np.arange(8)[:, None] * np.arange(ROWS)[None, :])
    coarse = np.stack([np.cos(angle), np.sin(angle)]).astype(np.float32)
    angle = -2 * np.pi * k / ROWS
    lanes = np.stack([np.cos(angle), np.sin(angle)]).astype(np.float32)
    lanes = np.broadcast_to(lanes[:, None, :], (2, 8, HALF)).copy()
    return first, second, octet, rows.copy(), between, shift, coarse, lanes


def lane_butterfly(real, imag, lanes_real, lanes_imag):
    low_r, high_r = real[:, :HALF], real[:, HALF:]
    low_i, high_i = imag[:, :HALF], imag[:, HALF:]
    sum_r, sum_i = low_r + high_r, low_i + high_i
    even_r = sum_r * lanes_real - sum_i * lanes_imag
    even_i = sum_r * lanes_imag + sum_i * lanes_real
    return even_r, even_i, low_r - high_r, low_i - high_i


def encode_kernel(core_ref, strain_ref, own_real_ref, own_imag_ref, other_real_ref, other_imag_ref, rows_ref):
    rows = rows_ref.shape[1]
    for which, out_refs in enumerate(((own_real_ref, own_imag_ref), (other_real_ref, other_imag_ref))):
        segment = core_ref[0] if which == 0 else 1 - core_ref[0]
        for part in range(2):
            for row in range(rows):
                rows_ref[part, row : row + 1, :] = strain_ref[segment, part : part + 1, row * ROWS : (row + 1) * ROWS]
        data = [rows_ref[0], rows_ref[1]]
        largest = jnp.max(jnp.maximum(jnp.abs(data[0]), jnp.abs(data[1])), axis=1, keepdims=True)
        exponent = jnp.floor(jnp.log2(jnp.maximum(largest, 1e-30)) + 1.001)
        scale = jnp.exp2(15.0 - exponent)
        for value, out_ref in zip(data, out_refs):
            number = jnp.clip(jnp.round(value * scale), -32767.0, 32767.0).astype(jnp.int32)
            packed = (number[:, :HALF] << 16) | (number[:, HALF:] & 0xFFFF)
            out_ref[0, 0:rows, :] = packed[:, :128]
            out_ref[0, rows : 2 * rows, :] = packed[:, 128:]
        spread = jnp.broadcast_to(exponent.astype(jnp.int32), (rows, 128))
        same = lax.broadcasted_iota(jnp.int32, (rows, 128), 0) == lax.broadcasted_iota(jnp.int32, (rows, 128), 1)
        line = jnp.sum(jnp.where(same, spread, 0), axis=0, keepdims=True)
        out_refs[0][0, 2 * rows :, :] = jnp.broadcast_to(line, (8, 128))


def encode(core, strain):
    rows = strain.shape[2] // ROWS
    real = jax.ShapeDtypeStruct((1, 2 * rows + 8, 128), jnp.int32)
    imag = jax.ShapeDtypeStruct((1, 2 * rows, 128), jnp.int32)
    return pl.pallas_call(
        encode_kernel,
        out_shape=(real, imag, real, imag),
        in_specs=[pl.BlockSpec(memory_space=pltpu.SMEM), pl.BlockSpec(memory_space=pltpu.VMEM)],
        out_specs=(pl.BlockSpec(memory_space=pltpu.VMEM),) * 4,
        scratch_shapes=[pltpu.VMEM((2, rows, ROWS), jnp.float32)],
    )(core.reshape(1), strain)


def make_kernel(slots, real_masks, imag_masks):
    blocks = [len(masks) for masks in (real_masks, imag_masks)]

    def kernel(*refs):
        plan_ref, edge_ref, own_ref, mate_ref = refs[:4]
        real_refs = refs[4 : 4 + blocks[0]]
        imag_refs = refs[4 + blocks[0] : 4 + sum(blocks)]
        (first_ref, second_ref, octet_ref, rows_ref, base_ref, shift_ref, coarse_ref, lanes_ref, out_ref, strain_ref,
         wave_ref, between_ref, qa_ref, qb_ref, pa_ref, pb_ref, xa_ref, xb_ref, o_ref, l_ref, z_ref, fold_ref, peak_ref, power_ref, sem) = refs[4 + sum(blocks) :]
        q_refs, p_refs, x_refs = (qa_ref, qb_ref), (pa_ref, pb_ref), (xa_ref, xb_ref)
        live = plan_ref[slots]
        own_count = plan_ref[slots + 1]
        device = plan_ref[slots + 2]

        def fetch(step):
            slot = plan_ref[step]
            buffer = step % 2

            @pl.when(step < own_count)
            def _():
                pltpu.make_async_copy(own_ref.at[slot], wave_ref.at[buffer], sem.at[buffer]).start()

            @pl.when(step >= own_count)
            def _():
                pltpu.make_async_copy(mate_ref.at[slot - slots // 2], wave_ref.at[buffer], sem.at[buffer]).start()

        fetch(0)
        out_ref[...] = jnp.zeros_like(out_ref)

        held = imag_refs[0].shape[1] // 2
        same = lax.broadcasted_iota(jnp.int32, (held, 128), 0) == lax.broadcasted_iota(jnp.int32, (held, 128), 1)
        for part, (part_refs, masks) in enumerate(((real_refs, real_masks), (imag_refs, imag_masks))):
            for ref, group in zip(part_refs, masks):
                for i, mask in enumerate(group):
                    row = pl.multiple_of((device ^ mask) * held, held)
                    if part == 0:
                        line = jnp.broadcast_to(ref[i, 2 * held : 2 * held + 1, :], (held, 128))
                        exponent = jnp.sum(jnp.where(same, line, 0).astype(jnp.float32), axis=1, keepdims=True)
                        scale = jnp.broadcast_to(jnp.exp2(exponent - 15.0), (held, 128))
                        strain_ref[2, pl.ds(row, held), 0:128] = scale
                    scale = strain_ref[2, pl.ds(row, held), 0:128]
                    for tile in range(2):
                        word = ref[i, tile * held : (tile + 1) * held, :]
                        high = (word >> 16).astype(jnp.float32) * scale
                        low = ((word << 16) >> 16).astype(jnp.float32) * scale
                        strain_ref[part, pl.ds(row, held), tile * 128 : tile * 128 + 128] = high
                        strain_ref[part, pl.ds(row, held), HALF + tile * 128 : HALF + tile * 128 + 128] = low

        for v in range(4):
            for mirror in range(2):
                at = mirror * 4 + v
                base_r = base_ref[0]
                base_i = base_ref[1] if mirror == 0 else -base_ref[1]
                shift_r = shift_ref[0, at : at + 1, :]
                shift_i = shift_ref[1, at : at + 1, :]
                between_ref[v, mirror, 0] = base_r * shift_r - base_i * shift_i
                between_ref[v, mirror, 1] = base_r * shift_i + base_i * shift_r

        def edges_of(step):
            base = plan_ref[step] * (BINS + 1)
            return edge_ref[base], edge_ref[base + BINS]

        def arrive(step, buffer):
            pltpu.make_async_copy(own_ref.at[0], wave_ref.at[buffer], sem.at[buffer]).wait()
            first_edge, last_edge = edges_of(step)

            def trim(r):
                start = r * ROWS

                @pl.when((start < first_edge) | (start + 16 * ROWS > last_edge))
                def _():
                    index = lax.broadcasted_iota(jnp.int32, (16, ROWS), 0) * ROWS + lax.broadcasted_iota(
                        jnp.int32, (16, ROWS), 1
                    )
                    inside = (index >= first_edge - start) & (index < last_edge - start)
                    for part in range(2):
                        wave = wave_ref[buffer, part, pl.ds(r, 16), :].astype(jnp.float32)
                        wave_ref[buffer, part, pl.ds(r, 16), :] = jnp.where(inside, wave, 0.0).astype(jnp.bfloat16)

            def clear(c, carry):
                trim(pl.multiple_of(c * 16, 16))
                return carry

            lax.fori_loop(0, first_edge // (16 * ROWS) + 1, clear, 0)
            lax.fori_loop(last_edge // (16 * ROWS), ROWS // 16, clear, 0)

        def front(c, buffer):
            q_ref, p_ref, x_ref = q_refs[buffer], p_refs[buffer], x_refs[buffer]

            def product(r, lane):
                data_r = strain_ref[0, pl.ds(r, 16), lane : lane + 128]
                data_i = strain_ref[1, pl.ds(r, 16), lane : lane + 128]
                wave_r = wave_ref[buffer, 0, pl.ds(r, 16), lane : lane + 128].astype(jnp.float32)
                wave_i = wave_ref[buffer, 1, pl.ds(r, 16), lane : lane + 128].astype(jnp.float32)
                real = data_r * wave_r + data_i * wave_i
                imag = data_i * wave_r - data_r * wave_i
                q_ref[0, pl.ds(r, 16), lane : lane + 128] = real
                q_ref[1, pl.ds(r, 16), lane : lane + 128] = imag
                p_ref[pl.ds(r, 16), lane : lane + 128] = wave_r * wave_r + wave_i * wave_i
                return real, imag

            r = c * 16 if isinstance(c, int) else pl.multiple_of(c * 16, 16)
            above = r + HALF if isinstance(c, int) else pl.multiple_of(r + HALF, 16)
            for lane in range(0, ROWS, 128):
                low_r, low_i = product(r, lane)
                high_r, high_i = product(above, lane)
                mixed = [
                    (low_r + high_r, low_i + high_i),
                    (low_r - high_i, low_i + high_r),
                    (low_r - high_r, low_i - high_i),
                    (low_r + high_i, low_i - high_r),
                ]
                for v in range(4):
                    real, imag = mixed[v]
                    if v != 2:
                        at = (1, 0, 0, 0)[v]
                        cosine = rows_ref[at, 0, pl.ds(r, 16), :]
                        sine = rows_ref[at, 1, pl.ds(r, 16), :]
                        if v == 3:
                            real, imag = real * cosine - imag * sine, real * sine + imag * cosine
                        else:
                            real, imag = real * cosine + imag * sine, imag * cosine - real * sine
                    for part, value in ((0, real), (1, imag)):
                        high, low = split_bf16(value)
                        column = (2 * v + part) * ROWS + lane
                        x_ref[pl.ds(r, 16), column : column + 128] = high
                        x_ref[pl.ds(above, 16), column : column + 128] = low

        arrive(0, 0)

        @pl.when(live > 1)
        def _():
            fetch(1)

        def first_front(c, carry):
            front(c, 0)
            return carry

        lax.fori_loop(0, HALF // 16, first_front, 0)

        def one_slot(step, buffer):
            q_ref, p_ref, x_ref = q_refs[buffer], p_refs[buffer], x_refs[buffer]
            slot = plan_ref[step]
            base = slot * (BINS + 1)

            @pl.when(step + 1 < live)
            def _():
                arrive(step + 1, 1 - buffer)

            @pl.when(step + 2 < live)
            def _():
                fetch(step + 2)

            offset = lax.broadcasted_iota(jnp.int32, (8, ROWS), 0) * ROWS + lax.broadcasted_iota(
                jnp.int32, (8, ROWS), 1
            )
            for b in range(BINS):
                lower = edge_ref[base + b]
                upper = edge_ref[base + b + 1]

                def gather(i, carry, lower=lower, upper=upper):
                    real, imag, power = carry
                    r = pl.multiple_of(i * 8, 8)
                    start = i * (8 * ROWS)
                    mask = (offset >= lower - start) & (offset < upper - start)
                    real = real + jnp.where(mask, q_ref[0, pl.ds(r, 8), :], 0.0)
                    imag = imag + jnp.where(mask, q_ref[1, pl.ds(r, 8), :], 0.0)
                    power = power + jnp.where(mask, p_ref[pl.ds(r, 8), :], 0.0)
                    return real, imag, power

                zero = jnp.zeros((8, ROWS), jnp.float32)
                real, imag, power = lax.fori_loop(
                    lower // (8 * ROWS), (upper + (8 * ROWS - 1)) // (8 * ROWS), gather, (zero, zero, zero)
                )
                fold_ref[0:8, b * ROWS : (b + 1) * ROWS] = real
                fold_ref[8:16, b * ROWS : (b + 1) * ROWS] = imag
                power_ref[8 * b : 8 * b + 8, :] = (
                    power[:, :128] + power[:, 128:256] + power[:, 256:384] + power[:, 384:]
                )
            power = jnp.sum(jnp.sum(power_ref[...].reshape(BINS, 8, 128), axis=1), axis=1, keepdims=True)
            energy = jnp.sum(power, axis=0, keepdims=True)
            weight = jnp.broadcast_to(power / energy, (BINS, 128))
            inverse = jnp.broadcast_to(1.0 / (power + EPSILON), (BINS, 128))


            def rows_stage(v, j):
                column = v * 2 * ROWS + j * HALF
                o_ref[v % 2, :, j * HALF : (j + 1) * HALF] = jnp.dot(
                    first_ref[...],
                    jnp.concatenate([x_ref[:, column : column + HALF], x_ref[0:HALF, column : column + HALF]], axis=0),
                    preferred_element_type=jnp.float32,
                )

            def middle(v, chunk):
                u = chunk * CHUNK
                cos_r = o_ref[v % 2, u : u + CHUNK, :ROWS]
                cos_i = o_ref[v % 2, u : u + CHUNK, ROWS:]
                sin_r = o_ref[v % 2, QUART + u : QUART + u + CHUNK, :ROWS]
                sin_i = o_ref[v % 2, QUART + u : QUART + u + CHUNK, ROWS:]
                for mirror in range(2):
                    if mirror == 0:
                        real, imag = cos_r - sin_i, cos_i + sin_r
                    else:
                        real, imag = cos_r + sin_i, cos_i - sin_r
                    cosine = between_ref[v, mirror, 0, u : u + CHUNK, :]
                    sine = between_ref[v, mirror, 1, u : u + CHUNK, :]
                    real, imag = real * cosine - imag * sine, real * sine + imag * cosine
                    values = lane_butterfly(real, imag, lanes_ref[0, 0:1, :], lanes_ref[1, 0:1, :])
                    for part in range(4):
                        high, low = split_bf16(values[part])
                        at = ((chunk * 2 + mirror) * 4 + part) * CHUNK
                        l_ref[v % 2, at : at + CHUNK, :HALF] = high
                        l_ref[v % 2, at : at + CHUNK, HALF:] = low

            def columns_stage(v, chunk):
                at = chunk * 8 * CHUNK
                z_ref[v % 2, at : at + 8 * CHUNK, :] = jnp.dot(
                    jnp.concatenate(
                        [l_ref[v % 2, at : at + 8 * CHUNK, :], l_ref[v % 2, at : at + 8 * CHUNK, :HALF]], axis=1
                    ),
                    second_ref[...],
                    preferred_element_type=jnp.float32,
                )

            def finish(v, chunk):
                for mirror in range(2):
                    cell = chunk if mirror == 0 else 7 - chunk
                    for parity in range(2):
                        at = ((chunk * 2 + mirror) * 4 + parity * 2) * CHUNK
                        real = z_ref[v % 2, at : at + CHUNK, :]
                        imag = z_ref[v % 2, at + CHUNK : at + 2 * CHUNK, :]
                        a, d = real[:, :128], real[:, 128:]
                        c, e = imag[:, :128], imag[:, 128:]
                        for side in range(2):
                            if side == 0:
                                re, im = a - e, c + d
                            else:
                                re, im = a + e, c - d
                            square = re * re + im * im
                            best = jnp.max(square.reshape(CHUNK // 8, 8, 128), axis=0)
                            lane = (parity * 2 + side) * 128
                            if v:
                                best = jnp.maximum(best, peak_ref[cell, :, lane : lane + 128])
                            peak_ref[cell, :, lane : lane + 128] = best

            chunks = list(range(HALF // 16))
            for turn in range(6):
                for j in range(4):
                    if chunks:
                        front(chunks.pop(0), 1 - buffer)
                    if 1 <= turn < 5:
                        middle(turn - 1, j)
                    if turn < 4:
                        rows_stage(turn, j)
                    if 2 <= turn:
                        columns_stage(turn - 2, j)
                    if 2 <= turn:
                        finish(turn - 2, j)

            coarse_r = jnp.concatenate([coarse_ref[0], coarse_ref[0]], axis=0)
            coarse_i = jnp.concatenate([coarse_ref[1], coarse_ref[1]], axis=0)
            for b in range(0, BINS, 2):
                high, low = split_bf16(fold_ref[:, b * ROWS : (b + 2) * ROWS])
                bands = jnp.dot(
                    octet_ref[...], jnp.concatenate([high, low, high], axis=0), preferred_element_type=jnp.float32
                )
                real = jnp.concatenate([bands[0:8, :ROWS], bands[0:8, ROWS:]], axis=0)
                imag = jnp.concatenate([bands[8:16, :ROWS], bands[8:16, ROWS:]], axis=0)
                real, imag = real * coarse_r - imag * coarse_i, real * coarse_i + imag * coarse_r
                values = lane_butterfly(real, imag, lanes_ref[0, 0:1, :], lanes_ref[1, 0:1, :])
                for part in range(4):
                    high, low = split_bf16(values[part])
                    at = part * 128 + b * 8
                    l_ref[0, at : at + 16, :HALF] = high
                    l_ref[0, at : at + 16, HALF:] = low
            z_ref[0, 0:512, :] = jnp.dot(
                jnp.concatenate([l_ref[0, 0:512, :], l_ref[0, 0:512, :HALF]], axis=1),
                second_ref[...],
                preferred_element_type=jnp.float32,
            )
            loud = jnp.concatenate(
                [jnp.max(peak_ref[cell], axis=0, keepdims=True) for cell in range(8)], axis=0
            )
            top = jnp.zeros((8, 128), jnp.float32)
            for parity in range(2):
                real = z_ref[0, parity * 256 : parity * 256 + 128, :]
                imag = z_ref[0, parity * 256 + 128 : parity * 256 + 256, :]
                a, d = real[:, :128], real[:, 128:]
                c, e = imag[:, :128], imag[:, 128:]
                for side in range(2):
                    if side == 0:
                        re, im = a - e, c + d
                    else:
                        re, im = a + e, c - d
                    re = re.reshape(BINS, 8, 128)
                    im = im.reshape(BINS, 8, 128)
                    total_r = jnp.sum(re, axis=0)
                    total_i = jnp.sum(im, axis=0)
                    misfit = jnp.zeros((8, 128), jnp.float32)
                    for b in range(BINS):
                        error_r = re[b] - weight[b : b + 1] * total_r
                        error_i = im[b] - weight[b : b + 1] * total_i
                        misfit = misfit + (error_r * error_r + error_i * error_i) * inverse[b : b + 1]
                    reduced = misfit / (2 * BINS - 2)
                    factor = jnp.where(
                        reduced > 1.0, jnp.exp(jnp.log((1.0 + reduced * reduced * reduced) / 2.0) * (-1.0 / 6.0)), 1.0
                    )
                    lane = (parity * 2 + side) * 128
                    top = jnp.maximum(top, jnp.sqrt(loud[:, lane : lane + 128]) * factor)
            best = jnp.max(top, axis=(0, 1), keepdims=True) / jnp.sqrt(energy)
            out_ref[pl.ds(slot, 1), :] = jnp.broadcast_to(best, (1, 128))

        def pair(i, carry):
            one_slot(2 * i, 0)

            @pl.when(2 * i + 1 < live)
            def _():
                one_slot(2 * i + 1, 1)

            return carry

        lax.fori_loop(0, (live + 1) // 2, pair, 0)

    return kernel


def slot_peaks(plan, edges, own_waves, mate_waves, real_blocks, imag_blocks, real_masks, imag_masks):
    slots = 2 * own_waves.shape[0]
    tables = [jnp.asarray(table) for table in host_tables()]
    smem = pl.BlockSpec(memory_space=pltpu.SMEM)
    hbm = pl.BlockSpec(memory_space=pl.ANY)
    vmem = pl.BlockSpec(memory_space=pltpu.VMEM)
    return pl.pallas_call(
        make_kernel(slots, real_masks, imag_masks),
        out_shape=jax.ShapeDtypeStruct((slots, 128), jnp.float32),
        in_specs=[smem, smem, hbm, hbm] + [vmem] * (len(real_blocks) + len(imag_blocks) + len(tables)),
        out_specs=vmem,
        scratch_shapes=[
            pltpu.VMEM((3, ROWS, ROWS), jnp.float32),
            pltpu.VMEM((2, 2, ROWS, ROWS), jnp.bfloat16),
            pltpu.VMEM((4, 2, 2, QUART, ROWS), jnp.float32),
            pltpu.VMEM((2, ROWS, ROWS), jnp.float32),
            pltpu.VMEM((2, ROWS, ROWS), jnp.float32),
            pltpu.VMEM((ROWS, ROWS), jnp.float32),
            pltpu.VMEM((ROWS, ROWS), jnp.float32),
            pltpu.VMEM((ROWS, 8 * ROWS), jnp.bfloat16),
            pltpu.VMEM((ROWS, 8 * ROWS), jnp.bfloat16),
            pltpu.VMEM((2, HALF, 2 * ROWS), jnp.float32),
            pltpu.VMEM((2, 1024, ROWS), jnp.bfloat16),
            pltpu.VMEM((2, 1024, HALF), jnp.float32),
            pltpu.VMEM((16, BINS * ROWS), jnp.float32),
            pltpu.VMEM((8, 8, ROWS), jnp.float32),
            pltpu.VMEM((8 * BINS, 128), jnp.float32),
            pltpu.SemaphoreType.DMA((2,)),
        ],
        compiler_params=pltpu.CompilerParams(vmem_limit_bytes=48 << 20),
    )(plan, edges, own_waves, mate_waves, *real_blocks, *imag_blocks, *tables)


def exchange(x, bit):
    devices = lax.axis_size("bank")
    return lax.ppermute(x, "bank", [(i, i ^ bit) for i in range(devices)])


def per_device(strain, templates, counts, edges):
    devices = lax.axis_size("bank")
    device = lax.axis_index("bank").astype(jnp.int32)
    core = device % 2
    slots = templates.shape[0]
    bits = [1 << i for i in range(1, devices.bit_length() - 1)]
    orders = [bits[::-1], bits[:1] + bits[:0:-1]]

    own_real, own_imag, other_real, other_imag = encode(core, strain)
    current = [
        jnp.concatenate([own, exchange(other, 1)]) for own, other in ((own_real, other_real), (own_imag, other_imag))
    ]
    small = jnp.concatenate([counts, edges.reshape(-1)])
    mate_small = exchange(small, 1)
    templates, mate_small, *current = lax.optimization_barrier((templates, mate_small, *current))
    own_waves = templates.reshape(slots, 2, ROWS, ROWS)
    masks = [[0, 1], [0, 1]]
    for level in range(len(bits)):
        arrived = [exchange(current[half], orders[half][level]) for half in range(2)]
        added = [[m ^ orders[half][level] for m in masks[half]] for half in range(2)]
        if level + 1 < len(bits):
            current = [jnp.concatenate([current[half], arrived[half]]) for half in range(2)]
            masks = [masks[half] + added[half] for half in range(2)]
        if level + 2 == len(bits):
            own_waves, *current = lax.optimization_barrier((own_waves, *current))
            mate_waves = exchange(own_waves, 1)
    blocks = [[current[half], arrived[half]] for half in range(2)]
    block_masks = [[masks[half], added[half]] for half in range(2)]

    own_count = small[0]
    live = own_count + mate_small[0]
    ramp = jnp.minimum(jnp.arange(2 * slots, dtype=jnp.int32), live - 1)
    order = jnp.where(ramp < own_count, ramp, slots + ramp - own_count)
    plan = jnp.concatenate([order, live[None], own_count[None], device[None]]).astype(jnp.int32)
    all_edges = jnp.concatenate([small[1:], mate_small[1:]])
    peaks = slot_peaks(plan, all_edges, own_waves, mate_waves, *blocks, *block_masks)

    mine = lax.broadcasted_iota(jnp.int32, peaks.shape, 1) % 2 == core
    arrived = exchange(peaks, 1)
    swapped = jnp.concatenate([arrived[slots:], arrived[:slots]])
    both = jnp.where(mine, peaks, swapped)
    best = both
    for bit in bits:
        best = jnp.maximum(best, exchange(best, bit))
    return (both[:slots, :2], jnp.max(best, axis=0)[:2])


def solution(mesh):
    placed = (P("seg", None, "bank"), P("bank", None, None), P("bank"), P("bank", None))
    return jax.shard_map(
        per_device,
        mesh=mesh,
        in_specs=placed,
        out_specs=(P("bank", "seg"), P("seg")),
        check_vma=False,
    )
```
